32 devices in a mesh: groups: 2 (over x), depth: 16 (over z, y, core).
Axes of the slice: x: 2, y: 2, z: 4, core: 2. Of those that a mesh axis runs over, the one named last changes fastest.
Arguments:
- object_slices: bfloat16 [32, 2, 512, 512], P(('groups', 'depth')), parts along dimension 0, may hold values from -1 to 1, as said below
- probes: float32 [8, 2, 128, 128], P('groups'), parts along dimension 0, may hold values from -4 to 4
- measured: float32 [16, 128, 128], P('groups'), parts along dimension 0, may hold values from 0.05 to 5
- scan_offsets: int32 [16, 2], P('groups'), parts along dimension 0, may hold values from 0 to 384
- probe_ids: int32 [16], P('groups'), parts along dimension 0, may hold values from 0 to 3
Outputs:
- object_grad: bfloat16 [32, 2, 512, 512], P(('groups', 'depth')), parts along dimension 0
The draws below stay inside these ranges and needn't reach their ends.
There are 2 independent parts, one for each index of `groups`. The reference program is written for one: setup_inputs(seed, part) draws one part's arguments, and reference() takes and returns one part's arrays. A program takes and returns all parts, laid end to end along the dimension named above; each array names one. Nothing has to cross between parts.
Inputs may be any that keep to these rules, and one draw needn't show every extreme that they name: `scan_offsets`: row and column of the first pixel of each position's window in the object. `probe_ids`: the probe state used at each position. `object_slices`: real and imaginary parts of a transmission whose modulus is at most 1.
All inputs are finite; a program needn't handle non-finite values.
Results may differ from the reference program's by a relative error of at most 0.001.
Values sent between devices are 32-bit elements; how exact they have to be, the bound alone decides.
A program may use at most 64 MiB of HBM per device.

```python
import math
import jax
import jax.numpy as jnp
from jax import lax

WIN = 128
OBJ = 512
POS = 8
NPROBE = 4
NSLICE = 16


def draw_object_slices(key, part):
    key_damping, key_phase = jax.random.split(jax.random.fold_in(key, 17))
    damping = jax.random.uniform(key_damping, (NSLICE, OBJ, OBJ), jnp.float32, 0.0, 0.01)
    phase_shift = jax.random.uniform(key_phase, (NSLICE, OBJ, OBJ), jnp.float32, -1.0, 1.0)
    modulus = jnp.exp(-damping)
    return jnp.stack([modulus * jnp.cos(phase_shift), modulus * jnp.sin(phase_shift)], 1).astype(jnp.bfloat16)


def touch_ends(result, stream_key, low, largest):
    longest = result.shape.index(max(result.shape))
    spots = []
    for shift in (0, 1):
        where = [jax.random.randint(jax.random.fold_in(stream_key, axis), (), 0, length) for axis, length in enumerate(result.shape)]
        where[longest] = (where[longest] + shift) % result.shape[longest]
        spots.append(tuple(where))
    return result.at[spots[0]].set(low).at[spots[1]].set(largest)


def gaussian(rng, shape, deviation, reach, held_as=jnp.bfloat16):
    result = jax.random.normal(rng, shape, jnp.float32) * deviation
    return jnp.minimum(jnp.maximum(result, -reach), reach).astype(held_as)


def setup_inputs(seed: int = 0, part: int = 0) -> dict:
    splits = jax.random.split(jax.random.key(seed), 6)
    part_keys = jax.random.split(jax.random.fold_in(splits[5], part), 6)
    return {
        "object_slices": draw_object_slices(jax.random.fold_in(jax.random.fold_in(splits[5], part), 71), part),
        "probes": gaussian(part_keys[1], (NPROBE, 2, WIN, WIN), 0.7, 4.0, jnp.float32),
        "measured": jnp.clip(jnp.exp(jax.random.uniform(part_keys[2], (POS, WIN, WIN), jnp.float32, math.log(0.05), math.log(5.0))), 0.05, 5.0),
        "scan_offsets": touch_ends(jax.random.randint(part_keys[3], (POS, 2), 0, OBJ - WIN + 1), jax.random.fold_in(part_keys[3], 1), 0, OBJ - WIN).astype(jnp.int32),
        "probe_ids": touch_ends(jax.random.randint(part_keys[4], (POS,), 0, NPROBE), jax.random.fold_in(part_keys[4], 1), 0, NPROBE - 1).astype(jnp.int32),
    }


def dft_tables(length):
    ordinal = jnp.arange(length, dtype=jnp.int32)
    products = ordinal[:, None] * ordinal[None, :] % length
    phase_angle = products.astype(jnp.float32) * (2.0 * math.pi / length)
    factor = 1.0 / math.sqrt(length)
    return (jnp.cos(phase_angle) * factor, -jnp.sin(phase_angle) * factor)

def kernel_table(length):
    ordinal = jnp.arange(length, dtype=jnp.int32)
    spatial = jnp.where(ordinal < length // 2, ordinal, ordinal - length)
    squares = (spatial[:, None] * spatial[:, None] + spatial[None, :] * spatial[None, :]) % (2 * length)
    phase_angle = squares.astype(jnp.float32) * (math.pi / length)
    return (jnp.cos(phase_angle), -jnp.sin(phase_angle))

def matmul_last(values, table):
    return jnp.einsum('bxk,kc->bxc', values, table, precision=lax.Precision.HIGHEST)

def matmul_first(table, values):
    return jnp.einsum('rj,bjc->brc', table, values, precision=lax.Precision.HIGHEST)

def transform(field_in, table_real, table_imag):
    real_part = field_in[:, 0]
    imag_part = field_in[:, 1]
    mid_real = matmul_last(real_part, table_real) - matmul_last(imag_part, table_imag)
    mid_imag = matmul_last(real_part, table_imag) + matmul_last(imag_part, table_real)
    out_real = matmul_first(table_real, mid_real) - matmul_first(table_imag, mid_imag)
    out_imag = matmul_first(table_real, mid_imag) + matmul_first(table_imag, mid_real)
    return (out_real, out_imag)

def complex_mul(left_real, left_imag, right_real, right_imag):
    return (left_real * right_real - left_imag * right_imag, left_real * right_imag + left_imag * right_real)

def cut_windows(object_slab, offsets):
    zero_index = jnp.zeros((), jnp.int32)

    def one_window(corner):
        return lax.dynamic_slice(object_slab, (zero_index, corner[0].astype(jnp.int32), corner[1].astype(jnp.int32)), (2, WIN, WIN))
    return jax.vmap(one_window)(offsets)

def paint(grad_field, offsets):
    zero_index = jnp.zeros((), jnp.int32)

    def add_one(position, image):
        corner_at = (zero_index, offsets[position, 0].astype(jnp.int32), offsets[position, 1].astype(jnp.int32))
        current = lax.dynamic_slice(image, corner_at, (2, WIN, WIN))
        return lax.dynamic_update_slice(image, current + grad_field[position], corner_at)
    return lax.fori_loop(0, grad_field.shape[0], add_one, jnp.zeros((2, OBJ, OBJ), jnp.float32))

def reference(object_slices, probes, measured, scan_offsets, probe_ids):
    table_real, table_imag = dft_tables(WIN)
    kernel_real, kernel_imag = kernel_table(WIN)
    start_wave = probes[probe_ids].astype(jnp.float32)

    def propagate(field_in, kernel_sign):
        spec_real, spec_imag = transform(field_in, table_real, table_imag)
        mixed_real, mixed_imag = complex_mul(spec_real, spec_imag, kernel_real, kernel_sign * kernel_imag)
        mixed_wave = jnp.stack([mixed_real, mixed_imag], 1)
        return transform(mixed_wave, table_real, -table_imag)

    def exit_of(wave_in, object_slab):
        windows = cut_windows(object_slab, scan_offsets).astype(jnp.float32)
        exit_real, exit_imag = complex_mul(wave_in[:, 0], wave_in[:, 1], windows[:, 0], windows[:, 1])
        return jnp.stack([exit_real, exit_imag], 1)

    def forward_slice(wave_in, object_slab):
        out_real, out_imag = propagate(exit_of(wave_in, object_slab), 1.0)
        return (jnp.stack([out_real, out_imag], 1), wave_in)
    unused_wave, stored = lax.scan(forward_slice, start_wave, object_slices)
    exit_last = exit_of(stored[NSLICE - 1], object_slices[NSLICE - 1])
    far_real, far_imag = transform(exit_last, table_real, table_imag)
    excess = far_real * far_real + far_imag * far_imag - measured
    residue = jnp.stack([excess * far_real, excess * far_imag], 1)
    seed_real, seed_imag = transform(residue, table_real, -table_imag)
    seed_wave = jnp.stack([seed_real, seed_imag], 1)

    def backward_slice(back_wave, inputs):
        object_slab, wave_in = inputs
        windows = cut_windows(object_slab, scan_offsets).astype(jnp.float32)
        term_real = wave_in[:, 0] * back_wave[:, 0] + wave_in[:, 1] * back_wave[:, 1]
        term_imag = wave_in[:, 0] * back_wave[:, 1] - wave_in[:, 1] * back_wave[:, 0]
        image = paint(jnp.stack([term_real, term_imag], 1), scan_offsets)
        sent_real = windows[:, 0] * back_wave[:, 0] + windows[:, 1] * back_wave[:, 1]
        sent_imag = windows[:, 0] * back_wave[:, 1] - windows[:, 1] * back_wave[:, 0]
        sent_wave = jnp.stack([sent_real, sent_imag], 1)
        prev_real, prev_imag = propagate(sent_wave, -1.0)
        return (jnp.stack([prev_real, prev_imag], 1), image)
    unused_back, images = lax.scan(backward_slice, seed_wave, (object_slices, stored), reverse=True)
    return images.astype(jnp.bfloat16)
```

```python
import functools
import math

import jax
import jax.numpy as jnp
import ml_dtypes
import numpy as np
from jax import lax
from jax.experimental import pallas as pl
from jax.experimental.pallas import tpu as pltpu
from jax.sharding import PartitionSpec as P

MESH = pl.DeviceIdType.MESH


def split_table(table):
    high = table.astype(ml_dtypes.bfloat16)
    low = (table - high.astype(np.float64)).astype(ml_dtypes.bfloat16)
    return np.stack([high, low])


def right_left(matrix):
    real, imag = matrix.real, matrix.imag
    right = np.block([[real, imag], [-imag, real]])
    left = np.block([[real, -imag], [imag, real]])
    return np.stack([split_table(right), split_table(left)])


def tables(length):
    ordinal = np.arange(length)
    dft = np.exp(-2j * math.pi * (np.outer(ordinal, ordinal) % length) / length) / math.sqrt(length)
    spatial = np.where(ordinal < length // 2, ordinal, ordinal - length)
    chirp = np.exp(-1j * math.pi * (spatial * spatial % (2 * length)) / length)
    prop = (dft.conj() * chirp[None, :]) @ dft
    return np.stack([right_left(prop), right_left(dft)])


def split(values):
    high = values.astype(jnp.bfloat16)
    low = (values - high.astype(jnp.float32)).astype(jnp.bfloat16)
    return high, low


def dot(left, right):
    return jnp.dot(left, right, preferred_element_type=jnp.float32)


def two_sided(real, imag, table_ref, which):
    length = real.shape[0]
    high, low = split(jnp.concatenate([real, imag], axis=1))
    both = dot(jnp.concatenate([high, low], axis=0), table_ref[which, 0, 0])
    mid = both[:length] + both[length:] + dot(high, table_ref[which, 0, 1])
    stacked = jnp.concatenate([mid[:, :length], mid[:, length:]], axis=0)
    high, low = split(stacked)
    both = dot(table_ref[which, 1, 0], jnp.concatenate([high, low], axis=1))
    out = both[:, :length] + both[:, length:] + dot(table_ref[which, 1, 1], high)
    return out[:length], out[length:]


def complex_mul(left_real, left_imag, right_real, right_imag):
    return (
        left_real * right_real - left_imag * right_imag,
        left_real * right_imag + left_imag * right_real,
    )


def cut_kernel(offsets, ids, obj, probes, windows, start):
    positions, window = windows.shape[0], windows.shape[-1]
    side = obj.shape[-1]
    start[...] = probes[ids[lax.rem(lax.axis_index("depth"), positions)]]
    tall, wide = window + 16, 2 * window
    for position in range(positions):
        row, col = offsets[position, 0], offsets[position, 1]
        row_base = jnp.minimum((row >> 4) << 4, side - tall)
        col_base = jnp.minimum(col // window * window, side - wide)
        down, across = row - row_base, col - col_base
        down = jnp.where(down == 0, 0, tall - down)
        across = jnp.where(across == 0, 0, wide - across)
        for part in range(2):
            tile = obj[
                0, part,
                pl.ds(pl.multiple_of(row_base, 16), tall),
                pl.ds(pl.multiple_of(col_base, 128), wide),
            ].astype(jnp.float32)
            tile = pltpu.roll(tile, across, 1)[:, :window]
            windows[position, part] = pltpu.roll(tile, down, 0)[:window]


def chain_kernel(
    count, windows, start, measured, table,
    grads,
    win_in, waves, back_buf, grad_out, hop_out, hop_in,
    win_send, win_recv, grad_send, grad_recv, hop_send, hop_recv,
):
    positions, window = measured.shape[0], measured.shape[-1]
    me = lax.axis_index("depth")
    mine = lax.rem(me, positions)
    segment = me // positions
    first = segment * positions
    segments = count // positions
    last = segments - 1

    barrier = pltpu.get_barrier_semaphore()
    for step in range(1, positions):
        peer = first + lax.rem(mine + step, positions)
        pl.semaphore_signal(barrier, inc=1, device_id={"depth": peer}, device_id_type=MESH)

    @pl.when(segment < last)
    def _():
        pl.semaphore_signal(barrier, inc=1, device_id={"depth": me + positions}, device_id_type=MESH)

    @pl.when(segment > 0)
    def _():
        pl.semaphore_signal(barrier, inc=1, device_id={"depth": me - positions}, device_id_type=MESH)

    def win_copy(place):
        return pltpu.make_async_remote_copy(
            src_ref=windows.at[place], dst_ref=win_in.at[mine],
            send_sem=win_send.at[place], recv_sem=win_recv.at[mine],
            device_id={"depth": first + place}, device_id_type=MESH,
        )

    win_in[mine] = windows[mine]
    pl.semaphore_wait(
        barrier,
        positions - 1 + jnp.where(segment < last, 1, 0) + jnp.where(segment > 0, 1, 0),
    )
    for step in range(1, positions):
        win_copy(lax.rem(mine + step, positions)).start()

    def hop(which, peer):
        return pltpu.make_async_remote_copy(
            src_ref=hop_out.at[which], dst_ref=hop_in.at[which],
            send_sem=hop_send.at[which], recv_sem=hop_recv.at[which],
            device_id={"depth": peer}, device_id_type=MESH,
        )

    @pl.when(segment == 0)
    def _():
        waves[0] = start[...]

    @pl.when(segment > 0)
    def _():
        hop(0, me - positions).wait_recv()
        waves[0] = hop_in[0]

    def win_wait(slot):
        @pl.when(slot != mine)
        def _():
            pltpu.make_async_remote_copy(
                src_ref=windows.at[slot], dst_ref=win_in.at[slot],
                send_sem=win_send.at[slot], recv_sem=win_recv.at[slot],
                device_id={"depth": first + slot}, device_id_type=MESH,
            ).wait_recv()

    def exit_wave(slot):
        return complex_mul(waves[slot, 0], waves[slot, 1], win_in[slot, 0], win_in[slot, 1])

    def forward(slot, carry):
        win_wait(slot)
        real, imag = two_sided(*exit_wave(slot), table, 0)
        waves[slot + 1, 0] = real
        waves[slot + 1, 1] = imag
        return carry

    lax.fori_loop(0, positions - 1, forward, 0)
    win_wait(positions - 1)

    @pl.when(segment < last)
    def _():
        real, imag = two_sided(*exit_wave(positions - 1), table, 0)
        hop_out[0, 0] = real
        hop_out[0, 1] = imag
        hop(0, me + positions).start()
        hop(1, me + positions).wait_recv()
        back_buf[0] = hop_in[1, 0]
        back_buf[1] = hop_in[1, 1]

    @pl.when(segment == last)
    def _():
        far_real, far_imag = two_sided(*exit_wave(positions - 1), table, 1)
        excess = far_real * far_real + far_imag * far_imag - measured[mine]
        real, imag = two_sided(excess * far_real, -(excess * far_imag), table, 1)
        back_buf[0] = real
        back_buf[1] = imag

    def grad_copy(slot):
        return pltpu.make_async_remote_copy(
            src_ref=grad_out.at[slot], dst_ref=grads.at[mine],
            send_sem=grad_send.at[slot], recv_sem=grad_recv.at[mine],
            device_id={"depth": first + slot}, device_id_type=MESH,
        )

    def give(slot):
        real, imag = complex_mul(waves[slot, 0], waves[slot, 1], back_buf[0], back_buf[1])

        @pl.when(slot == mine)
        def _():
            grads[mine, 0] = real
            grads[mine, 1] = -imag

        @pl.when(slot != mine)
        def _():
            grad_out[slot, 0] = real
            grad_out[slot, 1] = -imag
            grad_copy(slot).start()

    def send_back(slot):
        return two_sided(
            *complex_mul(win_in[slot, 0], win_in[slot, 1], back_buf[0], back_buf[1]), table, 0
        )

    def backward(step, carry):
        slot = positions - 1 - step
        give(slot)
        real, imag = send_back(slot)
        back_buf[0] = real
        back_buf[1] = imag
        return carry

    lax.fori_loop(0, positions - 1, backward, 0)
    give(0)

    @pl.when(segment > 0)
    def _():
        real, imag = send_back(0)
        hop_out[1, 0] = real
        hop_out[1, 1] = imag
        hop(1, me - positions).start()
        hop(1, me - positions).wait_send()

    @pl.when(segment < last)
    def _():
        hop(0, me + positions).wait_send()

    for step in range(1, positions):
        win_copy(lax.rem(mine + step, positions)).wait_send()

    def finish(slot, carry):
        @pl.when(slot != mine)
        def _():
            grad_copy(slot).wait_send()
            pltpu.make_async_remote_copy(
                src_ref=grad_out.at[slot], dst_ref=grads.at[slot],
                send_sem=grad_send.at[slot], recv_sem=grad_recv.at[slot],
                device_id={"depth": first + slot}, device_id_type=MESH,
            ).wait_recv()

        return carry

    lax.fori_loop(0, positions, finish, 0)


def paint_kernel(offsets, grads, out, total):
    positions, window = grads.shape[0], grads.shape[-1]
    side = out.shape[-1]
    total[...] = jnp.zeros_like(total)
    tall, wide = window + 8, 2 * window
    for position in range(positions):
        row, col = offsets[position, 0], offsets[position, 1]
        row_base = jnp.minimum((row >> 3) << 3, side - tall)
        col_base = jnp.minimum(col // window * window, side - wide)
        rows = pl.ds(pl.multiple_of(row_base, 8), tall)
        cols = pl.ds(pl.multiple_of(col_base, 128), wide)
        for part in range(2):
            tile = grads[position, part]
            tile = jnp.concatenate([tile, jnp.zeros((8, window), jnp.float32)], axis=0)
            tile = pltpu.roll(tile, row - row_base, 0)
            tile = jnp.concatenate([tile, jnp.zeros((tall, window), jnp.float32)], axis=1)
            tile = pltpu.roll(tile, col - col_base, 1)
            total[part, rows, cols] += tile
    out[0] = total[...].astype(out.dtype)


def body(object_slices, probes, measured, scan_offsets, probe_ids, *, count):
    positions, window = measured.shape[0], measured.shape[-1]
    side = object_slices.shape[-1]
    assert count % positions == 0
    table = jnp.asarray(tables(window))
    vmem = pl.BlockSpec(memory_space=pltpu.VMEM)
    smem = pl.BlockSpec(memory_space=pltpu.SMEM)
    field = (2, window, window)
    stack = pltpu.VMEM((positions,) + field, jnp.float32)
    sems = pltpu.SemaphoreType.DMA((positions,))
    windows, start = pl.pallas_call(
        cut_kernel,
        out_shape=(
            jax.ShapeDtypeStruct((positions,) + field, jnp.float32),
            jax.ShapeDtypeStruct(field, jnp.float32),
        ),
        in_specs=[smem, smem, vmem, vmem],
        out_specs=(vmem, vmem),
        compiler_params=pltpu.CompilerParams(vmem_limit_bytes=16 * 1024 * 1024),
    )(scan_offsets, probe_ids, object_slices, probes)
    grads = pl.pallas_call(
        functools.partial(chain_kernel, count),
        out_shape=jax.ShapeDtypeStruct((positions,) + field, jnp.float32),
        in_specs=[vmem, vmem, vmem, vmem],
        out_specs=vmem,
        scratch_shapes=[
            stack, stack,
            pltpu.VMEM(field, jnp.float32),
            stack,
            pltpu.VMEM((2,) + field, jnp.float32),
            pltpu.VMEM((2,) + field, jnp.float32),
            sems, sems, sems, sems,
            pltpu.SemaphoreType.DMA((2,)),
            pltpu.SemaphoreType.DMA((2,)),
        ],
        compiler_params=pltpu.CompilerParams(
            collective_id=0, has_side_effects=True, vmem_limit_bytes=40 * 1024 * 1024
        ),
    )(windows, start, measured, table)
    return pl.pallas_call(
        paint_kernel,
        out_shape=jax.ShapeDtypeStruct(object_slices.shape, jnp.bfloat16),
        in_specs=[smem, vmem],
        out_specs=vmem,
        scratch_shapes=[pltpu.VMEM((2, side, side), jnp.float32)],
        compiler_params=pltpu.CompilerParams(vmem_limit_bytes=16 * 1024 * 1024),
    )(scan_offsets, grads)


def solution(mesh):
    return jax.shard_map(
        functools.partial(body, count=mesh.shape["depth"]),
        mesh=mesh,
        in_specs=(
            P(("groups", "depth"), None, None, None),
            P("groups", None, None, None),
            P("groups", None, None),
            P("groups", None),
            P("groups"),
        ),
        out_specs=P(("groups", "depth"), None, None, None),
        check_vma=False,
    )
```

```python
import functools
import math

import jax
import jax.numpy as jnp
import ml_dtypes
import numpy as np
from jax import lax
from jax.experimental import pallas as pl
from jax.experimental.pallas import tpu as pltpu
from jax.sharding import PartitionSpec as P

MESH = pl.DeviceIdType.MESH


def split_table(table):
    high = table.astype(ml_dtypes.bfloat16)
    low = (table - high.astype(np.float64)).astype(ml_dtypes.bfloat16)
    return np.stack([high, low])


def right_left(matrix):
    real, imag = matrix.real, matrix.imag
    right = np.block([[real, imag], [-imag, real]])
    left = np.block([[real, -imag], [imag, real]])
    return np.stack([split_table(right), split_table(left)])


def tables(length):
    ordinal = np.arange(length)
    dft = np.exp(-2j * math.pi * (np.outer(ordinal, ordinal) % length) / length) / math.sqrt(length)
    spatial = np.where(ordinal < length // 2, ordinal, ordinal - length)
    chirp = np.exp(-1j * math.pi * (spatial * spatial % (2 * length)) / length)
    prop = (dft.conj() * chirp[None, :]) @ dft
    return np.stack([right_left(prop), right_left(dft)])


def split(values):
    high = values.astype(jnp.bfloat16)
    low = (values - high.astype(jnp.float32)).astype(jnp.bfloat16)
    return high, low


def dot(left, right):
    return jnp.dot(left, right, preferred_element_type=jnp.float32)


def two_sided(real, imag, table_ref, which):
    length = real.shape[0]
    high, low = split(jnp.concatenate([real, imag], axis=1))
    both = dot(jnp.concatenate([high, low], axis=0), table_ref[which, 0, 0])
    mid = both[:length] + both[length:] + dot(high, table_ref[which, 0, 1])
    stacked = jnp.concatenate([mid[:, :length], mid[:, length:]], axis=0)
    high, low = split(stacked)
    both = dot(table_ref[which, 1, 0], jnp.concatenate([high, low], axis=1))
    out = both[:, :length] + both[:, length:] + dot(table_ref[which, 1, 1], high)
    return out[:length], out[length:]


def complex_mul(left_real, left_imag, right_real, right_imag):
    return (
        left_real * right_real - left_imag * right_imag,
        left_real * right_imag + left_imag * right_real,
    )


def one_hot(length, width, start, axis):
    shape = (length, width) if axis == 0 else (width, length)
    place = lax.broadcasted_iota(jnp.int32, shape, axis)
    wanted = lax.broadcasted_iota(jnp.int32, shape, 1 - axis) + start
    return jnp.where(place == wanted, 1.0, 0.0).astype(jnp.bfloat16)


def chain_kernel(
    count, offsets, ids, obj, probes, measured, table_hbm,
    grads,
    table, windows, win_in, waves, back_buf, grad_out, hop_out, hop_in,
    win_send, win_recv, grad_send, grad_recv, hop_send, hop_recv, table_sem,
):
    positions, window = measured.shape[0], measured.shape[-1]
    me = lax.axis_index("depth")
    mine = lax.rem(me, positions)
    segment = me // positions
    first = segment * positions
    segments = count // positions
    last = segments - 1

    table_copy = pltpu.make_async_copy(table_hbm, table, table_sem)
    table_copy.start()
    barrier = pltpu.get_barrier_semaphore()
    for step in range(1, positions):
        peer = first + lax.rem(mine + step, positions)
        pl.semaphore_signal(barrier, inc=1, device_id={"depth": peer}, device_id_type=MESH)

    @pl.when(segment < last)
    def _():
        pl.semaphore_signal(barrier, inc=1, device_id={"depth": me + positions}, device_id_type=MESH)

    @pl.when(segment > 0)
    def _():
        pl.semaphore_signal(barrier, inc=1, device_id={"depth": me - positions}, device_id_type=MESH)

    def win_copy(place):
        return pltpu.make_async_remote_copy(
            src_ref=windows.at[place], dst_ref=win_in.at[mine],
            send_sem=win_send.at[place], recv_sem=win_recv.at[mine],
            device_id={"depth": first + place}, device_id_type=MESH,
        )

    side = obj.shape[-1]
    field = obj[0].reshape(2 * side, side)
    for pair in range(0, positions, 2):
        places = [lax.rem(mine + pair + 1 + i, positions) for i in range(2)]
        across = [one_hot(side, window, offsets[place, 1], 0) for place in places]
        strips = dot(field, jnp.concatenate(across, axis=1)).astype(jnp.bfloat16)
        for i, place in enumerate(places):
            strip = strips[:, i * window : (i + 1) * window]
            strip = jnp.concatenate([strip[:side], strip[side:]], axis=1)
            tile = dot(one_hot(side, window, offsets[place, 0], 1), strip)
            target = win_in if pair + i + 1 == positions else windows
            target[place, 0] = tile[:, :window]
            target[place, 1] = tile[:, window:]
        if pair == 0:
            pl.semaphore_wait(
                barrier,
                positions - 1 + jnp.where(segment < last, 1, 0) + jnp.where(segment > 0, 1, 0),
            )
        for i, place in enumerate(places):
            if pair + i + 1 < positions:
                win_copy(place).start()
    table_copy.wait()

    def hop(which, peer):
        return pltpu.make_async_remote_copy(
            src_ref=hop_out.at[which], dst_ref=hop_in.at[which],
            send_sem=hop_send.at[which], recv_sem=hop_recv.at[which],
            device_id={"depth": peer}, device_id_type=MESH,
        )

    @pl.when(segment == 0)
    def _():
        chosen = ids[mine]
        wave = jnp.zeros(probes.shape[1:], jnp.float32)
        for which in range(probes.shape[0]):
            wave = jnp.where(chosen == which, probes[which], wave)
        waves[0] = wave

    @pl.when(segment > 0)
    def _():
        hop(0, me - positions).wait_recv()
        waves[0] = hop_in[0]

    def win_wait(slot):
        @pl.when(slot != mine)
        def _():
            pltpu.make_async_remote_copy(
                src_ref=windows.at[slot], dst_ref=win_in.at[slot],
                send_sem=win_send.at[slot], recv_sem=win_recv.at[slot],
                device_id={"depth": first + slot}, device_id_type=MESH,
            ).wait_recv()

    def exit_wave(slot):
        return complex_mul(waves[slot, 0], waves[slot, 1], win_in[slot, 0], win_in[slot, 1])

    def forward(slot, carry):
        win_wait(slot)
        real, imag = two_sided(*exit_wave(slot), table, 0)
        waves[slot + 1, 0] = real
        waves[slot + 1, 1] = imag
        return carry

    lax.fori_loop(0, positions - 1, forward, 0)
    win_wait(positions - 1)

    @pl.when(segment < last)
    def _():
        real, imag = two_sided(*exit_wave(positions - 1), table, 0)
        hop_out[0, 0] = real
        hop_out[0, 1] = imag
        hop(0, me + positions).start()
        hop(1, me + positions).wait_recv()
        back_buf[0] = hop_in[1, 0]
        back_buf[1] = hop_in[1, 1]

    @pl.when(segment == last)
    def _():
        far_real, far_imag = two_sided(*exit_wave(positions - 1), table, 1)
        excess = far_real * far_real + far_imag * far_imag - measured[mine]
        real, imag = two_sided(excess * far_real, -(excess * far_imag), table, 1)
        back_buf[0] = real
        back_buf[1] = imag

    def grad_copy(slot):
        return pltpu.make_async_remote_copy(
            src_ref=grad_out.at[slot], dst_ref=grads.at[mine],
            send_sem=grad_send.at[slot], recv_sem=grad_recv.at[mine],
            device_id={"depth": first + slot}, device_id_type=MESH,
        )

    def give(slot):
        real, imag = complex_mul(waves[slot, 0], waves[slot, 1], back_buf[0], back_buf[1])

        @pl.when(slot == mine)
        def _():
            grads[mine, 0] = real
            grads[mine, 1] = -imag

        @pl.when(slot != mine)
        def _():
            grad_out[slot, 0] = real
            grad_out[slot, 1] = -imag
            grad_copy(slot).start()

    def send_back(slot):
        return two_sided(
            *complex_mul(win_in[slot, 0], win_in[slot, 1], back_buf[0], back_buf[1]), table, 0
        )

    def backward(step, carry):
        slot = positions - 1 - step
        give(slot)
        real, imag = send_back(slot)
        back_buf[0] = real
        back_buf[1] = imag
        return carry

    lax.fori_loop(0, positions - 1, backward, 0)
    give(0)

    @pl.when(segment > 0)
    def _():
        real, imag = send_back(0)
        hop_out[1, 0] = real
        hop_out[1, 1] = imag
        hop(1, me - positions).start()
        hop(1, me - positions).wait_send()

    @pl.when(segment < last)
    def _():
        hop(0, me + positions).wait_send()

    for step in range(1, positions):
        win_copy(lax.rem(mine + step, positions)).wait_send()

    def finish(slot, carry):
        @pl.when(slot != mine)
        def _():
            grad_copy(slot).wait_send()
            pltpu.make_async_remote_copy(
                src_ref=grad_out.at[slot], dst_ref=grads.at[slot],
                send_sem=grad_send.at[slot], recv_sem=grad_recv.at[slot],
                device_id={"depth": first + slot}, device_id_type=MESH,
            ).wait_recv()

        return carry

    lax.fori_loop(0, positions, finish, 0)


def paint_kernel(offsets, grads, out, total):
    positions, window = grads.shape[0], grads.shape[-1]
    side = out.shape[-1]
    total[...] = jnp.zeros_like(total)
    tall, wide = window + 8, 2 * window
    for position in range(positions):
        row, col = offsets[position, 0], offsets[position, 1]
        row_base = jnp.minimum((row >> 3) << 3, side - tall)
        col_base = jnp.minimum(col // window * window, side - wide)
        rows = pl.ds(pl.multiple_of(row_base, 8), tall)
        cols = pl.ds(pl.multiple_of(col_base, 128), wide)
        for part in range(2):
            tile = grads[position, part]
            tile = jnp.concatenate([tile, jnp.zeros((8, window), jnp.float32)], axis=0)
            tile = pltpu.roll(tile, row - row_base, 0)
            tile = jnp.concatenate([tile, jnp.zeros((tall, window), jnp.float32)], axis=1)
            tile = pltpu.roll(tile, col - col_base, 1)
            total[part, rows, cols] += tile
    out[0] = total[...].astype(out.dtype)


def body(object_slices, probes, measured, scan_offsets, probe_ids, *, count):
    positions, window = measured.shape[0], measured.shape[-1]
    side = object_slices.shape[-1]
    assert count % positions == 0
    table = jnp.asarray(tables(window))
    vmem = pl.BlockSpec(memory_space=pltpu.VMEM)
    smem = pl.BlockSpec(memory_space=pltpu.SMEM)
    field = (2, window, window)
    stack = pltpu.VMEM((positions,) + field, jnp.float32)
    sems = pltpu.SemaphoreType.DMA((positions,))
    grads = pl.pallas_call(
        functools.partial(chain_kernel, count),
        out_shape=jax.ShapeDtypeStruct((positions,) + field, jnp.float32),
        in_specs=[smem, smem, vmem, vmem, vmem, pl.BlockSpec(memory_space=pl.ANY)],
        out_specs=vmem,
        scratch_shapes=[
            pltpu.VMEM(table.shape, jnp.bfloat16),
            stack, stack, stack,
            pltpu.VMEM(field, jnp.float32),
            stack,
            pltpu.VMEM((2,) + field, jnp.float32),
            pltpu.VMEM((2,) + field, jnp.float32),
            sems, sems, sems, sems,
            pltpu.SemaphoreType.DMA((2,)),
            pltpu.SemaphoreType.DMA((2,)),
            pltpu.SemaphoreType.DMA,
        ],
        compiler_params=pltpu.CompilerParams(
            collective_id=0, has_side_effects=True, vmem_limit_bytes=40 * 1024 * 1024
        ),
    )(scan_offsets, probe_ids, object_slices, probes, measured, table)
    return pl.pallas_call(
        paint_kernel,
        out_shape=jax.ShapeDtypeStruct(object_slices.shape, jnp.bfloat16),
        in_specs=[smem, vmem],
        out_specs=vmem,
        scratch_shapes=[pltpu.VMEM((2, side, side), jnp.float32)],
        compiler_params=pltpu.CompilerParams(vmem_limit_bytes=16 * 1024 * 1024),
    )(scan_offsets, grads)


def solution(mesh):
    return jax.shard_map(
        functools.partial(body, count=mesh.shape["depth"]),
        mesh=mesh,
        in_specs=(
            P(("groups", "depth"), None, None, None),
            P("groups", None, None, None),
            P("groups", None, None),
            P("groups", None),
            P("groups"),
        ),
        out_specs=P(("groups", "depth"), None, None, None),
        check_vma=False,
    )
```

```python
import functools
import math

import jax
import jax.numpy as jnp
import ml_dtypes
import numpy as np
from jax import lax
from jax.experimental import pallas as pl
from jax.experimental.pallas import tpu as pltpu
from jax.sharding import PartitionSpec as P

MESH = pl.DeviceIdType.MESH


def split_table(table):
    high = table.astype(ml_dtypes.bfloat16)
    low = (table - high.astype(np.float64)).astype(ml_dtypes.bfloat16)
    return np.stack([high, low])


def right_left(matrix):
    real, imag = matrix.real, matrix.imag
    right = np.block([[real, imag], [-imag, real]])
    left = np.block([[real, -imag], [imag, real]])
    return np.stack([split_table(right), split_table(left)])


def tables(length):
    ordinal = np.arange(length)
    dft = np.exp(-2j * math.pi * (np.outer(ordinal, ordinal) % length) / length) / math.sqrt(length)
    spatial = np.where(ordinal < length // 2, ordinal, ordinal - length)
    chirp = np.exp(-1j * math.pi * (spatial * spatial % (2 * length)) / length)
    prop = (dft.conj() * chirp[None, :]) @ dft
    return np.stack([right_left(prop), right_left(dft)])


def split(values):
    high = values.astype(jnp.bfloat16)
    low = (values - high.astype(jnp.float32)).astype(jnp.bfloat16)
    return high, low


def dot(left, right):
    return jnp.dot(left, right, preferred_element_type=jnp.float32)


def two_sided(real, imag, table_ref, which):
    length = real.shape[0]
    high, low = split(jnp.concatenate([real, imag], axis=1))
    both = dot(jnp.concatenate([high, low], axis=0), table_ref[which, 0, 0])
    mid = both[:length] + both[length:] + dot(high, table_ref[which, 0, 1])
    stacked = jnp.concatenate([mid[:, :length], mid[:, length:]], axis=0)
    high, low = split(stacked)
    both = dot(table_ref[which, 1, 0], jnp.concatenate([high, low], axis=1))
    out = both[:, :length] + both[:, length:] + dot(table_ref[which, 1, 1], high)
    return out[:length], out[length:]


def complex_mul(left_real, left_imag, right_real, right_imag):
    return (
        left_real * right_real - left_imag * right_imag,
        left_real * right_imag + left_imag * right_real,
    )


def one_hot(length, width, start, axis):
    shape = (length, width) if axis == 0 else (width, length)
    place = lax.broadcasted_iota(jnp.int32, shape, axis)
    wanted = lax.broadcasted_iota(jnp.int32, shape, 1 - axis) + start
    return jnp.where(place == wanted, 1.0, 0.0).astype(jnp.bfloat16)


def chain_kernel(
    count, shift, offsets, ids, obj_hbm, probes_hbm, measured_hbm, table_hbm,
    grads,
    table, obj, probes, measured, windows, win_in, waves, back_buf, grad_out, hop_out, hop_in,
    win_send, win_recv, grad_send, grad_recv, hop_send, hop_recv, load_sem,
):
    positions, window = measured_hbm.shape[0], measured_hbm.shape[-1]
    me = lax.axis_index("depth")
    mine = lax.rem(me, positions)
    segment = me // positions
    last = count // positions - 1

    loads = [
        pltpu.make_async_copy(source, target, load_sem.at[i])
        for i, (source, target) in enumerate((
            (obj_hbm.at[0], obj), (table_hbm, table), (probes_hbm, probes),
            (measured_hbm.at[mine], measured),
        ))
    ]
    for load in loads:
        load.start()

    def lead(place):
        return shift * (1 - 2 * lax.rem(place, 2))

    def begin(part, place):
        return jnp.where(part == 0, 0, part * positions - lead(place))

    def holder(place):
        return jnp.minimum(jnp.maximum(me + lead(place), 0) // positions, last)

    low = begin(segment, mine)
    slots = jnp.where(segment == last, count, begin(segment + 1, mine)) - low
    keeps = holder(mine) == segment
    early = (lax.rem(mine, 2) == 0) & (segment > 0)
    held_back = jnp.where(early, shift, 0)

    barrier = pltpu.get_barrier_semaphore()

    def greet(peer):
        pl.semaphore_signal(barrier, inc=1, device_id={"depth": peer}, device_id_type=MESH)

    def greet_owner(slot, carry):
        @pl.when(low + slot != me)
        def _():
            greet(low + slot)

        return carry

    lax.fori_loop(0, slots, greet_owner, 0)
    for step in range(1, positions):
        place = lax.rem(mine + step, positions)
        greet(holder(place) * positions + place)

    @pl.when(jnp.logical_not(keeps))
    def _():
        greet(holder(mine) * positions + mine)

    @pl.when(segment < last)
    def _():
        greet(me + positions)

    @pl.when(segment > 0)
    def _():
        greet(me - positions)

    greetings = (
        slots + positions - jnp.where(keeps, 2, 0)
        + jnp.where(segment < last, 1, 0) + jnp.where(segment > 0, 1, 0)
    )

    def win_copy(place):
        part = holder(place)
        slot = me - begin(part, place)
        return pltpu.make_async_remote_copy(
            src_ref=windows.at[place], dst_ref=win_in.at[slot],
            send_sem=win_send.at[place], recv_sem=win_recv.at[slot],
            device_id={"depth": part * positions + place}, device_id_type=MESH,
        )

    loads[0].wait()
    side = obj.shape[-1]
    field = obj[...].reshape(2 * side, side)
    for pair in range(0, positions, 2):
        places = [lax.rem(mine + pair + 1 + i, positions) for i in range(2)]
        across = [one_hot(side, window, offsets[place, 1], 0) for place in places]
        strips = dot(field, jnp.concatenate(across, axis=1)).astype(jnp.bfloat16)
        for i, place in enumerate(places):
            strip = strips[:, i * window : (i + 1) * window]
            strip = jnp.concatenate([strip[:side], strip[side:]], axis=1)
            tile = dot(one_hot(side, window, offsets[place, 0], 1), strip)
            windows[place, 0] = tile[:, :window]
            windows[place, 1] = tile[:, window:]
        if pair == 0:
            pl.semaphore_wait(barrier, greetings)
        for i, place in enumerate(places):
            if pair + i + 1 < positions:
                win_copy(place).start()

    @pl.when(keeps)
    def _():
        win_in[me - low] = windows[mine]

    @pl.when(jnp.logical_not(keeps))
    def _():
        win_copy(mine).start()

    for load in loads[1:]:
        load.wait()

    def hop(which, peer):
        return pltpu.make_async_remote_copy(
            src_ref=hop_out.at[which], dst_ref=hop_in.at[which],
            send_sem=hop_send.at[which], recv_sem=hop_recv.at[which],
            device_id={"depth": peer}, device_id_type=MESH,
        )

    @pl.when(segment == 0)
    def _():
        chosen = ids[mine]
        wave = jnp.zeros(probes.shape[1:], jnp.float32)
        for which in range(probes.shape[0]):
            wave = jnp.where(chosen == which, probes[which], wave)
        waves[0] = wave

    @pl.when(segment > 0)
    def _():
        hop(0, me - positions).wait_recv()
        waves[0] = hop_in[0]

    def win_wait(slot):
        @pl.when(low + slot != me)
        def _():
            pltpu.make_async_remote_copy(
                src_ref=windows.at[0], dst_ref=win_in.at[slot],
                send_sem=win_send.at[0], recv_sem=win_recv.at[slot],
                device_id={"depth": low + slot}, device_id_type=MESH,
            ).wait_recv()

    def exit_wave(slot):
        return complex_mul(waves[slot, 0], waves[slot, 1], win_in[slot, 0], win_in[slot, 1])

    def forward(slot, carry):
        win_wait(slot)
        real, imag = two_sided(*exit_wave(slot), table, 0)
        waves[slot + 1, 0] = real
        waves[slot + 1, 1] = imag
        return carry

    lax.fori_loop(0, slots - 1, forward, 0)
    win_wait(slots - 1)

    @pl.when(segment < last)
    def _():
        real, imag = two_sided(*exit_wave(slots - 1), table, 0)
        hop_out[0, 0] = real
        hop_out[0, 1] = imag
        hop(0, me + positions).start()
        hop(1, me + positions).wait_recv()
        back_buf[0] = hop_in[1, 0]
        back_buf[1] = hop_in[1, 1]

    @pl.when(segment == last)
    def _():
        far_real, far_imag = two_sided(*exit_wave(slots - 1), table, 1)
        excess = far_real * far_real + far_imag * far_imag - measured[...]
        real, imag = two_sided(excess * far_real, -(excess * far_imag), table, 1)
        back_buf[0] = real
        back_buf[1] = imag

    def grad_copy(slot):
        return pltpu.make_async_remote_copy(
            src_ref=grad_out.at[slot], dst_ref=grads.at[mine],
            send_sem=grad_send.at[slot], recv_sem=grad_recv.at[mine],
            device_id={"depth": low + slot}, device_id_type=MESH,
        )

    def give(slot):
        real, imag = complex_mul(waves[slot, 0], waves[slot, 1], back_buf[0], back_buf[1])

        @pl.when(low + slot == me)
        def _():
            grads[mine, 0] = real
            grads[mine, 1] = -imag

        @pl.when(low + slot != me)
        def _():
            grad_out[slot, 0] = real
            grad_out[slot, 1] = -imag

            @pl.when(slot >= held_back)
            def _():
                grad_copy(slot).start()

    def send_back(slot):
        return two_sided(
            *complex_mul(win_in[slot, 0], win_in[slot, 1], back_buf[0], back_buf[1]), table, 0
        )

    def backward(step, carry):
        slot = slots - 1 - step
        give(slot)
        real, imag = send_back(slot)
        back_buf[0] = real
        back_buf[1] = imag
        return carry

    lax.fori_loop(0, slots - 1, backward, 0)
    give(0)

    @pl.when(segment > 0)
    def _():
        real, imag = send_back(0)
        hop_out[1, 0] = real
        hop_out[1, 1] = imag
        hop(1, me - positions).start()
        hop(1, me - positions).wait_send()

    @pl.when(segment < last)
    def _():
        hop(0, me + positions).wait_send()

    @pl.when(early)
    def _():
        for slot in range(shift):
            grad_copy(slot).start()

    def sent(slot, carry):
        @pl.when(low + slot != me)
        def _():
            grad_copy(slot).wait_send()

        return carry

    lax.fori_loop(0, slots, sent, 0)

    def landed(place):
        win_copy(place).wait_send()
        pltpu.make_async_remote_copy(
            src_ref=grad_out.at[0], dst_ref=grads.at[place],
            send_sem=grad_send.at[0], recv_sem=grad_recv.at[place],
            device_id={"depth": holder(place) * positions + place}, device_id_type=MESH,
        ).wait_recv()

    for step in range(1, positions):
        landed(lax.rem(mine + step, positions))

    @pl.when(jnp.logical_not(keeps))
    def _():
        landed(mine)


def paint_kernel(offsets, grads, out, total):
    positions, window = grads.shape[0], grads.shape[-1]
    side = out.shape[-1]
    total[...] = jnp.zeros_like(total)
    tall, wide = window + 8, 2 * window
    for position in range(positions):
        row, col = offsets[position, 0], offsets[position, 1]
        row_base = jnp.minimum((row >> 3) << 3, side - tall)
        col_base = jnp.minimum(col // window * window, side - wide)
        rows = pl.ds(pl.multiple_of(row_base, 8), tall)
        cols = pl.ds(pl.multiple_of(col_base, 128), wide)
        for part in range(2):
            tile = grads[position, part]
            tile = jnp.concatenate([tile, jnp.zeros((8, window), jnp.float32)], axis=0)
            tile = pltpu.roll(tile, row - row_base, 0)
            tile = jnp.concatenate([tile, jnp.zeros((tall, window), jnp.float32)], axis=1)
            tile = pltpu.roll(tile, col - col_base, 1)
            total[part, rows, cols] += tile
    out[0] = total[...].astype(out.dtype)


def body(object_slices, probes, measured, scan_offsets, probe_ids, *, count):
    positions, window = measured.shape[0], measured.shape[-1]
    side = object_slices.shape[-1]
    assert count % positions == 0
    table = jnp.asarray(tables(window))
    vmem = pl.BlockSpec(memory_space=pltpu.VMEM)
    smem = pl.BlockSpec(memory_space=pltpu.SMEM)
    field = (2, window, window)
    shift = positions // 4
    stack = pltpu.VMEM((positions,) + field, jnp.float32)
    chain = pltpu.VMEM((positions + shift,) + field, jnp.float32)
    sems = pltpu.SemaphoreType.DMA((positions,))
    chain_sems = pltpu.SemaphoreType.DMA((positions + shift,))
    hbm = pl.BlockSpec(memory_space=pltpu.HBM)
    grads = pl.pallas_call(
        functools.partial(chain_kernel, count, shift),
        out_shape=jax.ShapeDtypeStruct((positions,) + field, jnp.float32),
        in_specs=[smem, smem, hbm, hbm, hbm, hbm],
        out_specs=vmem,
        scratch_shapes=[
            pltpu.VMEM(table.shape, jnp.bfloat16),
            pltpu.VMEM(object_slices.shape[1:], jnp.bfloat16),
            pltpu.VMEM(probes.shape, jnp.float32),
            pltpu.VMEM((window, window), jnp.float32),
            stack, chain, chain,
            pltpu.VMEM(field, jnp.float32),
            chain,
            pltpu.VMEM((2,) + field, jnp.float32),
            pltpu.VMEM((2,) + field, jnp.float32),
            sems, chain_sems, chain_sems, sems,
            pltpu.SemaphoreType.DMA((2,)),
            pltpu.SemaphoreType.DMA((2,)),
            pltpu.SemaphoreType.DMA((4,)),
        ],
        compiler_params=pltpu.CompilerParams(
            collective_id=0, has_side_effects=True, vmem_limit_bytes=40 * 1024 * 1024
        ),
    )(scan_offsets, probe_ids, object_slices, probes, measured, table)
    return pl.pallas_call(
        paint_kernel,
        out_shape=jax.ShapeDtypeStruct(object_slices.shape, jnp.bfloat16),
        in_specs=[smem, vmem],
        out_specs=vmem,
        scratch_shapes=[pltpu.VMEM((2, side, side), jnp.float32)],
        compiler_params=pltpu.CompilerParams(vmem_limit_bytes=16 * 1024 * 1024),
    )(scan_offsets, grads)


def solution(mesh):
    return jax.shard_map(
        functools.partial(body, count=mesh.shape["depth"]),
        mesh=mesh,
        in_specs=(
            P(("groups", "depth"), None, None, None),
            P("groups", None, None, None),
            P("groups", None, None),
            P("groups", None),
            P("groups"),
        ),
        out_specs=P(("groups", "depth"), None, None, None),
        check_vma=False,
    )
```

```python
import functools
import math

import jax
import jax.numpy as jnp
import ml_dtypes
import numpy as np
from jax import lax
from jax.experimental import pallas as pl
from jax.experimental.pallas import tpu as pltpu
from jax.sharding import PartitionSpec as P

MESH = pl.DeviceIdType.MESH


def split_table(table):
    high = table.astype(ml_dtypes.bfloat16)
    low = (table - high.astype(np.float64)).astype(ml_dtypes.bfloat16)
    return np.stack([high, low])


def right_left(matrix):
    real, imag = matrix.real, matrix.imag
    right = np.block([[real, imag], [-imag, real]])
    left = np.block([[real, -imag], [imag, real]])
    return np.stack([split_table(right), split_table(left)])


def tables(length):
    ordinal = np.arange(length)
    dft = np.exp(-2j * math.pi * (np.outer(ordinal, ordinal) % length) / length) / math.sqrt(length)
    spatial = np.where(ordinal < length // 2, ordinal, ordinal - length)
    chirp = np.exp(-1j * math.pi * (spatial * spatial % (2 * length)) / length)
    prop = (dft.conj() * chirp[None, :]) @ dft
    return np.stack([right_left(prop), right_left(dft)])


def split(values):
    high = values.astype(jnp.bfloat16)
    low = (values - high.astype(jnp.float32)).astype(jnp.bfloat16)
    return high, low


def dot(left, right):
    return jnp.dot(left, right, preferred_element_type=jnp.float32)


def two_sided(real, imag, table_ref, which):
    length = real.shape[0]
    high, low = split(jnp.concatenate([real, imag], axis=1))
    both = dot(jnp.concatenate([high, low], axis=0), table_ref[which, 0, 0])
    mid = both[:length] + both[length:] + dot(high, table_ref[which, 0, 1])
    stacked = jnp.concatenate([mid[:, :length], mid[:, length:]], axis=0)
    high, low = split(stacked)
    both = dot(table_ref[which, 1, 0], jnp.concatenate([high, low], axis=1))
    out = both[:, :length] + both[:, length:] + dot(table_ref[which, 1, 1], high)
    return out[:length], out[length:]


def complex_mul(left_real, left_imag, right_real, right_imag):
    return (
        left_real * right_real - left_imag * right_imag,
        left_real * right_imag + left_imag * right_real,
    )


def one_hot(length, width, start, axis):
    shape = (length, width) if axis == 0 else (width, length)
    place = lax.broadcasted_iota(jnp.int32, shape, axis)
    wanted = lax.broadcasted_iota(jnp.int32, shape, 1 - axis) + start
    return jnp.where(place == wanted, 1.0, 0.0).astype(jnp.bfloat16)


def chain_kernel(
    count, shift, offsets, ids, obj_hbm, probes_hbm, measured_hbm, table_hbm,
    grads,
    table, obj, probes, measured, windows, win_in, waves, back_buf, grad_out, hop_out, hop_in,
    win_send, win_recv, grad_send, grad_recv, hop_send, hop_recv, load_sem,
):
    positions, window = measured_hbm.shape[0], measured_hbm.shape[-1]
    me = lax.axis_index("depth")
    mine = lax.rem(me, positions)
    segment = me // positions
    last = count // positions - 1

    loads = [
        pltpu.make_async_copy(source, target, load_sem.at[i])
        for i, (source, target) in enumerate((
            (obj_hbm.at[0], obj), (table_hbm, table), (probes_hbm, probes),
            (measured_hbm.at[mine], measured),
        ))
    ]
    for load in loads:
        load.start()

    def lead(place):
        return shift * (1 - 2 * lax.rem(place, 2))

    def begin(part, place):
        return jnp.where(part == 0, 0, part * positions - lead(place))

    def holder(place):
        return jnp.minimum(jnp.maximum(me + lead(place), 0) // positions, last)

    low = begin(segment, mine)
    slots = jnp.where(segment == last, count, begin(segment + 1, mine)) - low
    keeps = holder(mine) == segment
    early = (lax.rem(mine, 2) == 0) & (segment > 0)
    held_back = jnp.where(early, shift, 0)

    barrier = pltpu.get_barrier_semaphore()

    def greet(peer):
        pl.semaphore_signal(barrier, inc=1, device_id={"depth": peer}, device_id_type=MESH)

    def greet_owner(slot, carry):
        @pl.when(low + slot != me)
        def _():
            greet(low + slot)

        return carry

    lax.fori_loop(0, slots, greet_owner, 0)
    for step in range(1, positions):
        place = lax.rem(mine + step, positions)
        greet(holder(place) * positions + place)

    @pl.when(jnp.logical_not(keeps))
    def _():
        greet(holder(mine) * positions + mine)

    @pl.when(segment < last)
    def _():
        greet(me + positions)

    @pl.when(segment > 0)
    def _():
        greet(me - positions)

    greetings = (
        slots + positions - jnp.where(keeps, 2, 0)
        + jnp.where(segment < last, 1, 0) + jnp.where(segment > 0, 1, 0)
    )

    def win_copy(place):
        part = holder(place)
        slot = me - begin(part, place)
        return pltpu.make_async_remote_copy(
            src_ref=windows.at[place], dst_ref=win_in.at[slot],
            send_sem=win_send.at[place], recv_sem=win_recv.at[slot],
            device_id={"depth": part * positions + place}, device_id_type=MESH,
        )

    loads[0].wait()
    side = obj.shape[-1]
    field = obj[...].reshape(2 * side, side)
    for pair in range(0, positions, 2):
        places = [lax.rem(mine + pair + 1 + i, positions) for i in range(2)]
        across = [one_hot(side, window, offsets[place, 1], 0) for place in places]
        strips = dot(field, jnp.concatenate(across, axis=1)).astype(jnp.bfloat16)
        for i, place in enumerate(places):
            strip = strips[:, i * window : (i + 1) * window]
            strip = jnp.concatenate([strip[:side], strip[side:]], axis=1)
            tile = dot(one_hot(side, window, offsets[place, 0], 1), strip)
            windows[place, 0] = tile[:, :window]
            windows[place, 1] = tile[:, window:]
        if pair == 0:
            pl.semaphore_wait(barrier, greetings)
        for i, place in enumerate(places):
            if pair + i + 1 < positions:
                win_copy(place).start()

    @pl.when(keeps)
    def _():
        win_in[me - low] = windows[mine]

    @pl.when(jnp.logical_not(keeps))
    def _():
        win_copy(mine).start()

    for load in loads[1:]:
        load.wait()

    def hop(which, peer):
        return pltpu.make_async_remote_copy(
            src_ref=hop_out.at[which], dst_ref=hop_in.at[which],
            send_sem=hop_send.at[which], recv_sem=hop_recv.at[which],
            device_id={"depth": peer}, device_id_type=MESH,
        )

    @pl.when(segment == 0)
    def _():
        chosen = ids[mine]
        wave = jnp.zeros(probes.shape[1:], jnp.float32)
        for which in range(probes.shape[0]):
            wave = jnp.where(chosen == which, probes[which], wave)
        waves[0] = wave

    @pl.when(segment > 0)
    def _():
        hop(0, me - positions).wait_recv()
        waves[0] = hop_in[0]

    def win_wait(slot):
        @pl.when(low + slot != me)
        def _():
            pltpu.make_async_remote_copy(
                src_ref=windows.at[0], dst_ref=win_in.at[slot],
                send_sem=win_send.at[0], recv_sem=win_recv.at[slot],
                device_id={"depth": low + slot}, device_id_type=MESH,
            ).wait_recv()

    def exit_wave(slot):
        return complex_mul(waves[slot, 0], waves[slot, 1], win_in[slot, 0], win_in[slot, 1])

    def forward(slot, carry):
        win_wait(slot)
        real, imag = two_sided(*exit_wave(slot), table, 0)
        waves[slot + 1, 0] = real
        waves[slot + 1, 1] = imag
        return carry

    lax.fori_loop(0, slots - 1, forward, 0)
    win_wait(slots - 1)

    @pl.when(segment < last)
    def _():
        real, imag = two_sided(*exit_wave(slots - 1), table, 0)
        hop_out[0, 0] = real
        hop_out[0, 1] = imag
        hop(0, me + positions).start()
        hop(1, me + positions).wait_recv()
        back_buf[0] = hop_in[1, 0]
        back_buf[1] = hop_in[1, 1]

    @pl.when(segment == last)
    def _():
        far_real, far_imag = two_sided(*exit_wave(slots - 1), table, 1)
        excess = far_real * far_real + far_imag * far_imag - measured[...]
        real, imag = two_sided(excess * far_real, -(excess * far_imag), table, 1)
        back_buf[0] = real
        back_buf[1] = imag

    def grad_copy(slot):
        return pltpu.make_async_remote_copy(
            src_ref=grad_out.at[slot], dst_ref=grads.at[mine],
            send_sem=grad_send.at[slot], recv_sem=grad_recv.at[mine],
            device_id={"depth": low + slot}, device_id_type=MESH,
        )

    def keep_copy(slot):
        return pltpu.make_async_copy(grad_out.at[slot], grads.at[mine], load_sem.at[0])

    def give(slot):
        real, imag = complex_mul(waves[slot, 0], waves[slot, 1], back_buf[0], back_buf[1])

        grad_out[slot, 0] = real
        grad_out[slot, 1] = -imag

        @pl.when(low + slot == me)
        def _():
            keep_copy(slot).start()

        @pl.when((low + slot != me) & (slot >= held_back))
        def _():
            grad_copy(slot).start()

    def send_back(slot):
        return two_sided(
            *complex_mul(win_in[slot, 0], win_in[slot, 1], back_buf[0], back_buf[1]), table, 0
        )

    def backward(step, carry):
        slot = slots - 1 - step
        give(slot)
        real, imag = send_back(slot)
        back_buf[0] = real
        back_buf[1] = imag
        return carry

    lax.fori_loop(0, slots - 1, backward, 0)
    give(0)

    @pl.when(segment > 0)
    def _():
        real, imag = send_back(0)
        hop_out[1, 0] = real
        hop_out[1, 1] = imag
        hop(1, me - positions).start()
        hop(1, me - positions).wait_send()

    @pl.when(segment < last)
    def _():
        hop(0, me + positions).wait_send()

    @pl.when(early)
    def _():
        for slot in range(shift):
            grad_copy(slot).start()

    def sent(slot, carry):
        @pl.when(low + slot != me)
        def _():
            grad_copy(slot).wait_send()

        @pl.when(low + slot == me)
        def _():
            keep_copy(slot).wait()

        return carry

    lax.fori_loop(0, slots, sent, 0)

    def landed(place):
        win_copy(place).wait_send()
        pltpu.make_async_remote_copy(
            src_ref=grad_out.at[0], dst_ref=grads.at[place],
            send_sem=grad_send.at[0], recv_sem=grad_recv.at[place],
            device_id={"depth": holder(place) * positions + place}, device_id_type=MESH,
        ).wait_recv()

    for step in range(1, positions):
        landed(lax.rem(mine + step, positions))

    @pl.when(jnp.logical_not(keeps))
    def _():
        landed(mine)


def paint_kernel(offsets, grads_hbm, out_hbm, grads, out, total, load_sem, store_sem):
    positions, window = grads.shape[0], grads.shape[-1]
    side = out.shape[-1]
    loads = [
        pltpu.make_async_copy(grads_hbm.at[i], grads.at[i], load_sem.at[i]) for i in range(positions)
    ]
    for load in loads:
        load.start()
    total[...] = jnp.zeros_like(total)
    tall, wide = window + 8, 2 * window
    for position in range(positions):
        loads[position].wait()
        row, col = offsets[position, 0], offsets[position, 1]
        row_base = jnp.minimum((row >> 3) << 3, side - tall)
        col_base = jnp.minimum(col // window * window, side - wide)
        rows = pl.ds(pl.multiple_of(row_base, 8), tall)
        cols = pl.ds(pl.multiple_of(col_base, 128), wide)
        for part in range(2):
            tile = grads[position, part]
            tile = jnp.concatenate([tile, jnp.zeros((8, window), jnp.float32)], axis=0)
            tile = pltpu.roll(tile, row - row_base, 0)
            tile = jnp.concatenate([tile, jnp.zeros((tall, window), jnp.float32)], axis=1)
            tile = pltpu.roll(tile, col - col_base, 1)
            total[part, rows, cols] += tile
    pieces = store_sem.shape[0]
    tall = side // pieces
    stores = []
    for piece in range(pieces):
        rows = pl.ds(piece * tall, tall)
        out[:, rows] = total[:, rows].astype(out.dtype)
        stores.append(
            pltpu.make_async_copy(out.at[:, rows], out_hbm.at[0, :, rows], store_sem.at[piece])
        )
        stores[-1].start()
    for store in stores:
        store.wait()


def body(object_slices, probes, measured, scan_offsets, probe_ids, *, count):
    positions, window = measured.shape[0], measured.shape[-1]
    side = object_slices.shape[-1]
    assert count % positions == 0
    table = jnp.asarray(tables(window))
    smem = pl.BlockSpec(memory_space=pltpu.SMEM)
    field = (2, window, window)
    shift = positions // 4
    stack = pltpu.VMEM((positions,) + field, jnp.float32)
    chain = pltpu.VMEM((positions + shift,) + field, jnp.float32)
    sems = pltpu.SemaphoreType.DMA((positions,))
    chain_sems = pltpu.SemaphoreType.DMA((positions + shift,))
    hbm = pl.BlockSpec(memory_space=pltpu.HBM)
    grads = pl.pallas_call(
        functools.partial(chain_kernel, count, shift),
        out_shape=jax.ShapeDtypeStruct((positions,) + field, jnp.float32),
        in_specs=[smem, smem, hbm, hbm, hbm, hbm],
        out_specs=hbm,
        scratch_shapes=[
            pltpu.VMEM(table.shape, jnp.bfloat16),
            pltpu.VMEM(object_slices.shape[1:], jnp.bfloat16),
            pltpu.VMEM(probes.shape, jnp.float32),
            pltpu.VMEM((window, window), jnp.float32),
            stack, chain, chain,
            pltpu.VMEM(field, jnp.float32),
            chain,
            pltpu.VMEM((2,) + field, jnp.float32),
            pltpu.VMEM((2,) + field, jnp.float32),
            sems, chain_sems, chain_sems, sems,
            pltpu.SemaphoreType.DMA((2,)),
            pltpu.SemaphoreType.DMA((2,)),
            pltpu.SemaphoreType.DMA((4,)),
        ],
        compiler_params=pltpu.CompilerParams(
            collective_id=0, has_side_effects=True, vmem_limit_bytes=58 * 1024 * 1024
        ),
    )(scan_offsets, probe_ids, object_slices, probes, measured, table)
    return pl.pallas_call(
        paint_kernel,
        out_shape=jax.ShapeDtypeStruct(object_slices.shape, jnp.bfloat16),
        in_specs=[smem, hbm],
        out_specs=hbm,
        scratch_shapes=[
            stack,
            pltpu.VMEM((2, side, side), jnp.bfloat16),
            pltpu.VMEM((2, side, side), jnp.float32),
            sems,
            pltpu.SemaphoreType.DMA((4,)),
        ],
        compiler_params=pltpu.CompilerParams(vmem_limit_bytes=58 * 1024 * 1024),
    )(scan_offsets, grads)


def solution(mesh):
    return jax.shard_map(
        functools.partial(body, count=mesh.shape["depth"]),
        mesh=mesh,
        in_specs=(
            P(("groups", "depth"), None, None, None),
            P("groups", None, None, None),
            P("groups", None, None),
            P("groups", None),
            P("groups"),
        ),
        out_specs=P(("groups", "depth"), None, None, None),
        check_vma=False,
    )
```

```python
import functools
import math

import jax
import jax.numpy as jnp
import ml_dtypes
import numpy as np
from jax import lax
from jax.experimental import pallas as pl
from jax.experimental.pallas import tpu as pltpu
from jax.sharding import PartitionSpec as P

MESH = pl.DeviceIdType.MESH


def split_table(table):
    high = table.astype(ml_dtypes.bfloat16)
    low = (table - high.astype(np.float64)).astype(ml_dtypes.bfloat16)
    return np.stack([high, low])


def right_left(matrix):
    real, imag = matrix.real, matrix.imag
    right = np.block([[real, imag], [-imag, real]])
    left = np.block([[real, -imag], [imag, real]])
    return np.stack([split_table(right), split_table(left)])


def tables(length):
    ordinal = np.arange(length)
    dft = np.exp(-2j * math.pi * (np.outer(ordinal, ordinal) % length) / length) / math.sqrt(length)
    spatial = np.where(ordinal < length // 2, ordinal, ordinal - length)
    chirp = np.exp(-1j * math.pi * (spatial * spatial % (2 * length)) / length)
    prop = (dft.conj() * chirp[None, :]) @ dft
    return np.stack([right_left(prop), right_left(dft)])


def split(values):
    high = values.astype(jnp.bfloat16)
    low = (values - high.astype(jnp.float32)).astype(jnp.bfloat16)
    return high, low


def dot(left, right):
    return jnp.dot(left, right, preferred_element_type=jnp.float32)


def two_sided(real, imag, table_ref, which):
    length = real.shape[0]
    high, low = split(jnp.concatenate([real, imag], axis=1))
    both = dot(jnp.concatenate([high, low], axis=0), table_ref[which, 0, 0])
    mid = both[:length] + both[length:] + dot(high, table_ref[which, 0, 1])
    stacked = jnp.concatenate([mid[:, :length], mid[:, length:]], axis=0)
    high, low = split(stacked)
    both = dot(table_ref[which, 1, 0], jnp.concatenate([high, low], axis=1))
    out = both[:, :length] + both[:, length:] + dot(table_ref[which, 1, 1], high)
    return out[:length], out[length:]


def complex_mul(left_real, left_imag, right_real, right_imag):
    return (
        left_real * right_real - left_imag * right_imag,
        left_real * right_imag + left_imag * right_real,
    )


def one_hot(length, width, start, axis):
    shape = (length, width) if axis == 0 else (width, length)
    place = lax.broadcasted_iota(jnp.int32, shape, axis)
    wanted = lax.broadcasted_iota(jnp.int32, shape, 1 - axis) + start
    return jnp.where(place == wanted, 1.0, 0.0).astype(jnp.bfloat16)


def chain_kernel(
    count, shift, offsets, ids, obj_hbm, probes_hbm, measured_hbm, table_hbm,
    grads,
    table, obj, probes, measured, windows, win_in, waves, back_buf, grad_out, hop_out, hop_in,
    win_send, win_recv, grad_send, grad_recv, hop_send, hop_recv, load_sem,
):
    positions, window = measured_hbm.shape[0], measured_hbm.shape[-1]
    me = lax.axis_index("depth")
    mine = lax.rem(me, positions)
    segment = me // positions
    last = count // positions - 1

    loads = [
        pltpu.make_async_copy(source, target, load_sem.at[i])
        for i, (source, target) in enumerate((
            (obj_hbm.at[0], obj), (table_hbm, table), (probes_hbm, probes),
            (measured_hbm.at[mine], measured),
        ))
    ]
    for load in loads:
        load.start()

    def lead(place):
        return shift * (1 - 2 * lax.rem(place, 2))

    def begin(part, place):
        return jnp.where(part == 0, 0, part * positions - lead(place))

    def holder(place):
        return jnp.minimum(jnp.maximum(me + lead(place), 0) // positions, last)

    low = begin(segment, mine)
    slots = jnp.where(segment == last, count, begin(segment + 1, mine)) - low
    keeps = holder(mine) == segment
    early = (lax.rem(mine, 2) == 0) & (segment > 0)
    held_back = jnp.where(early, shift, 0)

    barrier = pltpu.get_barrier_semaphore()

    def greet(peer):
        pl.semaphore_signal(barrier, inc=1, device_id={"depth": peer}, device_id_type=MESH)

    def greet_owner(slot, carry):
        @pl.when(low + slot != me)
        def _():
            greet(low + slot)

        return carry

    lax.fori_loop(0, slots, greet_owner, 0)
    for step in range(1, positions):
        place = lax.rem(mine + step, positions)
        greet(holder(place) * positions + place)

    @pl.when(jnp.logical_not(keeps))
    def _():
        greet(holder(mine) * positions + mine)

    @pl.when(segment < last)
    def _():
        greet(me + positions)

    @pl.when(segment > 0)
    def _():
        greet(me - positions)

    greetings = (
        slots + positions - jnp.where(keeps, 2, 0)
        + jnp.where(segment < last, 1, 0) + jnp.where(segment > 0, 1, 0)
    )

    def win_copy(place):
        part = holder(place)
        slot = me - begin(part, place)
        return pltpu.make_async_remote_copy(
            src_ref=windows.at[place], dst_ref=win_in.at[slot],
            send_sem=win_send.at[place], recv_sem=win_recv.at[slot],
            device_id={"depth": part * positions + place}, device_id_type=MESH,
        )

    loads[0].wait()
    side = obj.shape[-1]
    field = obj[...].reshape(2 * side, side)
    for pair in range(0, positions, 2):
        places = [lax.rem(mine + pair + 1 + i, positions) for i in range(2)]
        across = [one_hot(side, window, offsets[1, place], 0) for place in places]
        strips = dot(field, jnp.concatenate(across, axis=1)).astype(jnp.bfloat16)
        for i, place in enumerate(places):
            strip = strips[:, i * window : (i + 1) * window]
            strip = jnp.concatenate([strip[:side], strip[side:]], axis=1)
            tile = dot(one_hot(side, window, offsets[0, place], 1), strip)
            windows[place, 0] = tile[:, :window]
            windows[place, 1] = tile[:, window:]
        if pair == 0:
            pl.semaphore_wait(barrier, greetings)
        for i, place in enumerate(places):
            if pair + i + 1 < positions:
                win_copy(place).start()

    @pl.when(keeps)
    def _():
        win_in[me - low] = windows[mine]

    @pl.when(jnp.logical_not(keeps))
    def _():
        win_copy(mine).start()

    for load in loads[1:]:
        load.wait()

    def hop(which, peer):
        return pltpu.make_async_remote_copy(
            src_ref=hop_out.at[which], dst_ref=hop_in.at[which],
            send_sem=hop_send.at[which], recv_sem=hop_recv.at[which],
            device_id={"depth": peer}, device_id_type=MESH,
        )

    @pl.when(segment == 0)
    def _():
        chosen = ids[mine]
        wave = jnp.zeros(probes.shape[1:], jnp.float32)
        for which in range(probes.shape[0]):
            wave = jnp.where(chosen == which, probes[which], wave)
        waves[0] = wave

    @pl.when(segment > 0)
    def _():
        hop(0, me - positions).wait_recv()
        waves[0] = hop_in[0]

    def win_wait(slot):
        @pl.when(low + slot != me)
        def _():
            pltpu.make_async_remote_copy(
                src_ref=windows.at[0], dst_ref=win_in.at[slot],
                send_sem=win_send.at[0], recv_sem=win_recv.at[slot],
                device_id={"depth": low + slot}, device_id_type=MESH,
            ).wait_recv()

    def exit_wave(slot):
        return complex_mul(waves[slot, 0], waves[slot, 1], win_in[slot, 0], win_in[slot, 1])

    def advance(slot):
        real, imag = two_sided(*exit_wave(slot), table, 0)
        waves[slot + 1, 0] = real
        waves[slot + 1, 1] = imag

    def forward(pair, carry):
        win_wait(2 * pair + 1)
        win_wait(2 * pair + 2)
        advance(2 * pair + 1)
        advance(2 * pair + 2)
        return carry

    win_wait(0)
    advance(0)
    lax.fori_loop(0, slots // 2 - 1, forward, 0)
    win_wait(slots - 1)

    @pl.when(segment < last)
    def _():
        real, imag = two_sided(*exit_wave(slots - 1), table, 0)
        hop_out[0, 0] = real
        hop_out[0, 1] = imag
        hop(0, me + positions).start()
        hop(1, me + positions).wait_recv()
        back_buf[0] = hop_in[1, 0]
        back_buf[1] = hop_in[1, 1]

    @pl.when(segment == last)
    def _():
        far_real, far_imag = two_sided(*exit_wave(slots - 1), table, 1)
        excess = far_real * far_real + far_imag * far_imag - measured[...]
        real, imag = two_sided(excess * far_real, -(excess * far_imag), table, 1)
        back_buf[0] = real
        back_buf[1] = imag

    def grad_copy(slot):
        return pltpu.make_async_remote_copy(
            src_ref=grad_out.at[slot], dst_ref=grads.at[mine],
            send_sem=grad_send.at[slot], recv_sem=grad_recv.at[mine],
            device_id={"depth": low + slot}, device_id_type=MESH,
        )

    def keep_copy(slot):
        return pltpu.make_async_copy(grad_out.at[slot], grads.at[mine], load_sem.at[0])

    def keep_term(slot):
        real, imag = complex_mul(waves[slot, 0], waves[slot, 1], back_buf[0], back_buf[1])
        grad_out[slot, 0] = real
        grad_out[slot, 1] = -imag

    def give(slot):
        @pl.when(low + slot == me)
        def _():
            keep_copy(slot).start()

        @pl.when((low + slot != me) & (slot >= held_back))
        def _():
            grad_copy(slot).start()

    def send_back(slot):
        return two_sided(
            *complex_mul(win_in[slot, 0], win_in[slot, 1], back_buf[0], back_buf[1]), table, 0
        )

    def backward(step, carry):
        slot = slots - 1 - step
        keep_term(slot)
        real, imag = send_back(slot)
        back_buf[0] = real
        back_buf[1] = imag
        give(slot)
        return carry

    lax.fori_loop(0, slots - 1, backward, 0)
    keep_term(0)
    give(0)

    @pl.when(segment > 0)
    def _():
        real, imag = send_back(0)
        hop_out[1, 0] = real
        hop_out[1, 1] = imag
        hop(1, me - positions).start()
        hop(1, me - positions).wait_send()

    @pl.when(segment < last)
    def _():
        hop(0, me + positions).wait_send()

    @pl.when(early)
    def _():
        for slot in range(shift):
            grad_copy(slot).start()

    def sent(slot, carry):
        @pl.when(low + slot != me)
        def _():
            grad_copy(slot).wait_send()

        @pl.when(low + slot == me)
        def _():
            keep_copy(slot).wait()

        return carry

    lax.fori_loop(0, slots, sent, 0)

    def landed(place):
        win_copy(place).wait_send()
        pltpu.make_async_remote_copy(
            src_ref=grad_out.at[0], dst_ref=grads.at[place],
            send_sem=grad_send.at[0], recv_sem=grad_recv.at[place],
            device_id={"depth": holder(place) * positions + place}, device_id_type=MESH,
        ).wait_recv()

    for step in range(1, positions):
        landed(lax.rem(mine + step, positions))

    @pl.when(jnp.logical_not(keeps))
    def _():
        landed(mine)


def paint_kernel(offsets, grads_hbm, out_hbm, grads, out, total, load_sem, store_sem):
    positions, window = grads.shape[0], grads.shape[-1]
    side = out.shape[-1]
    loads = [
        pltpu.make_async_copy(grads_hbm.at[i], grads.at[i], load_sem.at[i]) for i in range(positions)
    ]
    for load in loads:
        load.start()
    total[...] = jnp.zeros_like(total)
    tall, wide = window + 8, 2 * window
    for position in range(positions):
        loads[position].wait()
        row, col = offsets[0, position], offsets[1, position]
        row_base = jnp.minimum((row >> 3) << 3, side - tall)
        col_base = jnp.minimum(col // window * window, side - wide)
        rows = pl.ds(pl.multiple_of(row_base, 8), tall)
        cols = pl.ds(pl.multiple_of(col_base, 128), wide)
        for part in range(2):
            tile = grads[position, part]
            tile = jnp.concatenate([tile, jnp.zeros((8, window), jnp.float32)], axis=0)
            tile = pltpu.roll(tile, row - row_base, 0)
            tile = jnp.concatenate([tile, jnp.zeros((tall, window), jnp.float32)], axis=1)
            tile = pltpu.roll(tile, col - col_base, 1)
            total[part, rows, cols] += tile
    pieces = store_sem.shape[0]
    tall = side // pieces
    stores = []
    for piece in range(pieces):
        rows = pl.ds(piece * tall, tall)
        out[:, rows] = total[:, rows].astype(out.dtype)
        stores.append(
            pltpu.make_async_copy(out.at[:, rows], out_hbm.at[0, :, rows], store_sem.at[piece])
        )
        stores[-1].start()
    for store in stores:
        store.wait()


def body(object_slices, probes, measured, scan_offsets, probe_ids, *, count):
    positions, window = measured.shape[0], measured.shape[-1]
    side = object_slices.shape[-1]
    assert count % positions == 0 and positions % 8 == 0
    table = jnp.asarray(tables(window))
    smem = pl.BlockSpec(memory_space=pltpu.SMEM)
    field = (2, window, window)
    shift = positions // 4
    stack = pltpu.VMEM((positions,) + field, jnp.float32)
    chain = pltpu.VMEM((positions + shift,) + field, jnp.float32)
    sems = pltpu.SemaphoreType.DMA((positions,))
    chain_sems = pltpu.SemaphoreType.DMA((positions + shift,))
    hbm = pl.BlockSpec(memory_space=pltpu.HBM)
    grads = pl.pallas_call(
        functools.partial(chain_kernel, count, shift),
        out_shape=jax.ShapeDtypeStruct((positions,) + field, jnp.float32),
        in_specs=[smem, smem, hbm, hbm, hbm, hbm],
        out_specs=hbm,
        scratch_shapes=[
            pltpu.VMEM(table.shape, jnp.bfloat16),
            pltpu.VMEM(object_slices.shape[1:], jnp.bfloat16),
            pltpu.VMEM(probes.shape, jnp.float32),
            pltpu.VMEM((window, window), jnp.float32),
            stack, chain, chain,
            pltpu.VMEM(field, jnp.float32),
            chain,
            pltpu.VMEM((2,) + field, jnp.float32),
            pltpu.VMEM((2,) + field, jnp.float32),
            sems, chain_sems, chain_sems, sems,
            pltpu.SemaphoreType.DMA((2,)),
            pltpu.SemaphoreType.DMA((2,)),
            pltpu.SemaphoreType.DMA((4,)),
        ],
        compiler_params=pltpu.CompilerParams(
            collective_id=0, has_side_effects=True, vmem_limit_bytes=58 * 1024 * 1024
        ),
    )(scan_offsets.T, probe_ids, object_slices, probes, measured, table)
    return pl.pallas_call(
        paint_kernel,
        out_shape=jax.ShapeDtypeStruct(object_slices.shape, jnp.bfloat16),
        in_specs=[smem, hbm],
        out_specs=hbm,
        scratch_shapes=[
            stack,
            pltpu.VMEM((2, side, side), jnp.bfloat16),
            pltpu.VMEM((2, side, side), jnp.float32),
            sems,
            pltpu.SemaphoreType.DMA((4,)),
        ],
        compiler_params=pltpu.CompilerParams(vmem_limit_bytes=58 * 1024 * 1024),
    )(scan_offsets.T, grads)


def solution(mesh):
    return jax.shard_map(
        functools.partial(body, count=mesh.shape["depth"]),
        mesh=mesh,
        in_specs=(
            P(("groups", "depth"), None, None, None),
            P("groups", None, None, None),
            P("groups", None, None),
            P("groups", None),
            P("groups"),
        ),
        out_specs=P(("groups", "depth"), None, None, None),
        check_vma=False,
    )
```

```python
import functools
import math

import jax
import jax.numpy as jnp
import ml_dtypes
import numpy as np
from jax import lax
from jax.experimental import pallas as pl
from jax.experimental.pallas import tpu as pltpu
from jax.sharding import PartitionSpec as P

MESH = pl.DeviceIdType.MESH


def split_table(table):
    high = table.astype(ml_dtypes.bfloat16)
    low = (table - high.astype(np.float64)).astype(ml_dtypes.bfloat16)
    return np.stack([high, low])


def right_left(matrix):
    real, imag = matrix.real, matrix.imag
    right = np.block([[real, imag], [-imag, real]])
    left = np.block([[real, -imag], [imag, real]])
    return np.stack([split_table(right), split_table(left)])


def tables(length):
    ordinal = np.arange(length)
    dft = np.exp(-2j * math.pi * (np.outer(ordinal, ordinal) % length) / length) / math.sqrt(length)
    spatial = np.where(ordinal < length // 2, ordinal, ordinal - length)
    chirp = np.exp(-1j * math.pi * (spatial * spatial % (2 * length)) / length)
    prop = (dft.conj() * chirp[None, :]) @ dft
    return np.stack([right_left(prop), right_left(dft)])


def split(values):
    high = values.astype(jnp.bfloat16)
    low = (values - high.astype(jnp.float32)).astype(jnp.bfloat16)
    return high, low


def dot(left, right):
    return jnp.dot(left, right, preferred_element_type=jnp.float32)


def two_sided(real, imag, table_ref, which):
    length = real.shape[0]
    high, low = split(jnp.concatenate([real, imag], axis=1))
    both = dot(jnp.concatenate([high, low], axis=0), table_ref[which, 0, 0])
    mid = both[:length] + both[length:] + dot(high, table_ref[which, 0, 1])
    stacked = jnp.concatenate([mid[:, :length], mid[:, length:]], axis=0)
    high, low = split(stacked)
    both = dot(table_ref[which, 1, 0], jnp.concatenate([high, low], axis=1))
    out = both[:, :length] + both[:, length:] + dot(table_ref[which, 1, 1], high)
    return out[:length], out[length:]


def complex_mul(left_real, left_imag, right_real, right_imag):
    return (
        left_real * right_real - left_imag * right_imag,
        left_real * right_imag + left_imag * right_real,
    )


def one_hot(length, width, start, axis):
    shape = (length, width) if axis == 0 else (width, length)
    place = lax.broadcasted_iota(jnp.int32, shape, axis)
    wanted = lax.broadcasted_iota(jnp.int32, shape, 1 - axis) + start
    return jnp.where(place == wanted, 1.0, 0.0).astype(jnp.bfloat16)


def chain_kernel(
    count, shift, offsets, ids, obj_hbm, probes_hbm, measured_hbm, table_hbm,
    grads,
    table, obj, probes, measured, windows, win_in, waves, back_buf, grad_out, hop_out, hop_in,
    win_send, win_recv, grad_send, grad_recv, hop_send, hop_recv, load_sem,
):
    positions, window = measured_hbm.shape[0], measured_hbm.shape[-1]
    me = lax.axis_index("depth")
    mine = lax.rem(me, positions)
    segment = me // positions
    last = count // positions - 1

    loads = [
        pltpu.make_async_copy(source, target, load_sem.at[i])
        for i, (source, target) in enumerate((
            (obj_hbm.at[0], obj), (table_hbm, table), (probes_hbm, probes),
            (measured_hbm.at[mine], measured),
        ))
    ]
    for load in loads:
        load.start()

    def lead(place):
        return shift * (1 - 2 * lax.rem(place, 2))

    def begin(part, place):
        return jnp.where(part == 0, 0, part * positions - lead(place))

    def holder(place):
        return jnp.minimum(jnp.maximum(me + lead(place), 0) // positions, last)

    low = begin(segment, mine)
    slots = jnp.where(segment == last, count, begin(segment + 1, mine)) - low
    keeps = holder(mine) == segment
    early = (lax.rem(mine, 2) == 0) & (segment > 0)
    held_back = jnp.where(early, shift, 0)

    barrier = pltpu.get_barrier_semaphore()

    def greet(peer):
        pl.semaphore_signal(barrier, inc=1, device_id={"depth": peer}, device_id_type=MESH)

    def greet_owner(slot, carry):
        @pl.when(low + slot != me)
        def _():
            greet(low + slot)

        return carry

    lax.fori_loop(0, slots, greet_owner, 0)
    for step in range(1, positions):
        place = lax.rem(mine + step, positions)
        greet(holder(place) * positions + place)

    @pl.when(jnp.logical_not(keeps))
    def _():
        greet(holder(mine) * positions + mine)

    @pl.when(segment < last)
    def _():
        greet(me + positions)

    @pl.when(segment > 0)
    def _():
        greet(me - positions)

    greetings = (
        slots + positions - jnp.where(keeps, 2, 0)
        + jnp.where(segment < last, 1, 0) + jnp.where(segment > 0, 1, 0)
    )

    def win_copy(place):
        part = holder(place)
        slot = me - begin(part, place)
        return pltpu.make_async_remote_copy(
            src_ref=windows.at[place], dst_ref=win_in.at[slot],
            send_sem=win_send.at[place], recv_sem=win_recv.at[slot],
            device_id={"depth": part * positions + place}, device_id_type=MESH,
        )

    loads[0].wait()
    side = obj.shape[-1]
    field = obj[...].reshape(2 * side, side)
    half = positions // 2

    def order(turn):
        return 2 * lax.rem(mine // 2 + 1 + turn % half, half) + turn // half

    def ship(place):
        @pl.when(jnp.logical_not(keeps & (place == mine)))
        def _():
            win_copy(place).start()

        @pl.when(keeps & (place == mine))
        def _():
            win_in[me - low] = windows[place]

    def shipped(place):
        @pl.when(jnp.logical_not(keeps & (place == mine)))
        def _():
            win_copy(place).wait_send()

    for pair in range(0, positions, 2):
        places = [order(pair), order(pair + 1)]
        across = [one_hot(side, window, offsets[1, place], 0) for place in places]
        strips = dot(field, jnp.concatenate(across, axis=1)).astype(jnp.bfloat16)
        for i, place in enumerate(places):
            strip = strips[:, i * window : (i + 1) * window]
            strip = jnp.concatenate([strip[:side], strip[side:]], axis=1)
            tile = dot(one_hot(side, window, offsets[0, place], 1), strip)
            windows[place, 0] = tile[:, :window]
            windows[place, 1] = tile[:, window:]
        if pair == 0:
            pl.semaphore_wait(barrier, greetings)
        if pair < half:
            for place in places:
                ship(place)
    for turn in range(half):
        shipped(order(turn))
    for turn in range(half, positions):
        ship(order(turn))

    for load in loads[1:]:
        load.wait()

    def hop(which, peer):
        return pltpu.make_async_remote_copy(
            src_ref=hop_out.at[which], dst_ref=hop_in.at[which],
            send_sem=hop_send.at[which], recv_sem=hop_recv.at[which],
            device_id={"depth": peer}, device_id_type=MESH,
        )

    @pl.when(segment == 0)
    def _():
        chosen = ids[mine]
        wave = jnp.zeros(probes.shape[1:], jnp.float32)
        for which in range(probes.shape[0]):
            wave = jnp.where(chosen == which, probes[which], wave)
        waves[0] = wave

    @pl.when(segment > 0)
    def _():
        hop(0, me - positions).wait_recv()
        waves[0] = hop_in[0]

    def win_wait(slot):
        @pl.when(low + slot != me)
        def _():
            pltpu.make_async_remote_copy(
                src_ref=windows.at[0], dst_ref=win_in.at[slot],
                send_sem=win_send.at[0], recv_sem=win_recv.at[slot],
                device_id={"depth": low + slot}, device_id_type=MESH,
            ).wait_recv()

    def exit_wave(slot):
        return complex_mul(waves[slot, 0], waves[slot, 1], win_in[slot, 0], win_in[slot, 1])

    def advance(slot):
        real, imag = two_sided(*exit_wave(slot), table, 0)
        waves[slot + 1, 0] = real
        waves[slot + 1, 1] = imag

    def forward(pair, carry):
        win_wait(2 * pair + 1)
        win_wait(2 * pair + 2)
        advance(2 * pair + 1)
        advance(2 * pair + 2)
        return carry

    win_wait(0)
    advance(0)
    lax.fori_loop(0, slots // 2 - 1, forward, 0)
    win_wait(slots - 1)

    @pl.when(segment < last)
    def _():
        real, imag = two_sided(*exit_wave(slots - 1), table, 0)
        hop_out[0, 0] = real
        hop_out[0, 1] = imag
        hop(0, me + positions).start()
        hop(1, me + positions).wait_recv()
        back_buf[0] = hop_in[1, 0]
        back_buf[1] = hop_in[1, 1]

    @pl.when(segment == last)
    def _():
        far_real, far_imag = two_sided(*exit_wave(slots - 1), table, 1)
        excess = far_real * far_real + far_imag * far_imag - measured[...]
        real, imag = two_sided(excess * far_real, -(excess * far_imag), table, 1)
        back_buf[0] = real
        back_buf[1] = imag

    def grad_copy(slot):
        return pltpu.make_async_remote_copy(
            src_ref=grad_out.at[slot], dst_ref=grads.at[mine],
            send_sem=grad_send.at[slot], recv_sem=grad_recv.at[mine],
            device_id={"depth": low + slot}, device_id_type=MESH,
        )

    def keep_copy(slot):
        return pltpu.make_async_copy(grad_out.at[slot], grads.at[mine], load_sem.at[0])

    def keep_term(slot):
        real, imag = complex_mul(waves[slot, 0], waves[slot, 1], back_buf[0], back_buf[1])
        grad_out[slot, 0] = real
        grad_out[slot, 1] = -imag

    def give(slot):
        @pl.when(low + slot == me)
        def _():
            keep_copy(slot).start()

        @pl.when((low + slot != me) & (slot >= held_back))
        def _():
            grad_copy(slot).start()

    def send_back(slot):
        return two_sided(
            *complex_mul(win_in[slot, 0], win_in[slot, 1], back_buf[0], back_buf[1]), table, 0
        )

    def backward(step, carry):
        slot = slots - 1 - step
        keep_term(slot)
        real, imag = send_back(slot)
        back_buf[0] = real
        back_buf[1] = imag
        give(slot)
        return carry

    lax.fori_loop(0, slots - 1, backward, 0)
    keep_term(0)
    give(0)

    @pl.when(segment > 0)
    def _():
        real, imag = send_back(0)
        hop_out[1, 0] = real
        hop_out[1, 1] = imag
        hop(1, me - positions).start()
        hop(1, me - positions).wait_send()

    @pl.when(segment < last)
    def _():
        hop(0, me + positions).wait_send()

    @pl.when(early)
    def _():
        for slot in range(shift):
            grad_copy(slot).start()

    def sent(slot, carry):
        @pl.when(low + slot != me)
        def _():
            grad_copy(slot).wait_send()

        @pl.when(low + slot == me)
        def _():
            keep_copy(slot).wait()

        return carry

    lax.fori_loop(0, slots, sent, 0)

    for turn in range(half, positions):
        shipped(order(turn))

    def landed(place):
        pltpu.make_async_remote_copy(
            src_ref=grad_out.at[0], dst_ref=grads.at[place],
            send_sem=grad_send.at[0], recv_sem=grad_recv.at[place],
            device_id={"depth": holder(place) * positions + place}, device_id_type=MESH,
        ).wait_recv()

    for step in range(1, positions):
        landed(lax.rem(mine + step, positions))

    @pl.when(jnp.logical_not(keeps))
    def _():
        landed(mine)


def paint_kernel(offsets, grads_hbm, out_hbm, grads, out, total, load_sem, store_sem):
    positions, window = grads.shape[0], grads.shape[-1]
    side = out.shape[-1]
    loads = [
        pltpu.make_async_copy(grads_hbm.at[i], grads.at[i], load_sem.at[i]) for i in range(positions)
    ]
    for load in loads:
        load.start()
    total[...] = jnp.zeros_like(total)
    tall, wide = window + 8, 2 * window
    for position in range(positions):
        loads[position].wait()
        row, col = offsets[0, position], offsets[1, position]
        row_base = jnp.minimum((row >> 3) << 3, side - tall)
        col_base = jnp.minimum(col // window * window, side - wide)
        rows = pl.ds(pl.multiple_of(row_base, 8), tall)
        cols = pl.ds(pl.multiple_of(col_base, 128), wide)
        for part in range(2):
            tile = grads[position, part]
            tile = jnp.concatenate([tile, jnp.zeros((8, window), jnp.float32)], axis=0)
            tile = pltpu.roll(tile, row - row_base, 0)
            tile = jnp.concatenate([tile, jnp.zeros((tall, window), jnp.float32)], axis=1)
            tile = pltpu.roll(tile, col - col_base, 1)
            total[part, rows, cols] += tile
    pieces = store_sem.shape[0]
    tall = side // pieces
    stores = []
    for piece in range(pieces):
        rows = pl.ds(piece * tall, tall)
        out[:, rows] = total[:, rows].astype(out.dtype)
        stores.append(
            pltpu.make_async_copy(out.at[:, rows], out_hbm.at[0, :, rows], store_sem.at[piece])
        )
        stores[-1].start()
    for store in stores:
        store.wait()


def body(object_slices, probes, measured, scan_offsets, probe_ids, *, count):
    positions, window = measured.shape[0], measured.shape[-1]
    side = object_slices.shape[-1]
    assert count % positions == 0 and positions % 8 == 0
    table = jnp.asarray(tables(window))
    smem = pl.BlockSpec(memory_space=pltpu.SMEM)
    field = (2, window, window)
    shift = positions // 4
    stack = pltpu.VMEM((positions,) + field, jnp.float32)
    chain = pltpu.VMEM((positions + shift,) + field, jnp.float32)
    sems = pltpu.SemaphoreType.DMA((positions,))
    chain_sems = pltpu.SemaphoreType.DMA((positions + shift,))
    hbm = pl.BlockSpec(memory_space=pltpu.HBM)
    grads = pl.pallas_call(
        functools.partial(chain_kernel, count, shift),
        out_shape=jax.ShapeDtypeStruct((positions,) + field, jnp.float32),
        in_specs=[smem, smem, hbm, hbm, hbm, hbm],
        out_specs=hbm,
        scratch_shapes=[
            pltpu.VMEM(table.shape, jnp.bfloat16),
            pltpu.VMEM(object_slices.shape[1:], jnp.bfloat16),
            pltpu.VMEM(probes.shape, jnp.float32),
            pltpu.VMEM((window, window), jnp.float32),
            stack, chain, chain,
            pltpu.VMEM(field, jnp.float32),
            chain,
            pltpu.VMEM((2,) + field, jnp.float32),
            pltpu.VMEM((2,) + field, jnp.float32),
            sems, chain_sems, chain_sems, sems,
            pltpu.SemaphoreType.DMA((2,)),
            pltpu.SemaphoreType.DMA((2,)),
            pltpu.SemaphoreType.DMA((4,)),
        ],
        compiler_params=pltpu.CompilerParams(
            collective_id=0, has_side_effects=True, vmem_limit_bytes=58 * 1024 * 1024
        ),
    )(scan_offsets.T, probe_ids, object_slices, probes, measured, table)
    return pl.pallas_call(
        paint_kernel,
        out_shape=jax.ShapeDtypeStruct(object_slices.shape, jnp.bfloat16),
        in_specs=[smem, hbm],
        out_specs=hbm,
        scratch_shapes=[
            stack,
            pltpu.VMEM((2, side, side), jnp.bfloat16),
            pltpu.VMEM((2, side, side), jnp.float32),
            sems,
            pltpu.SemaphoreType.DMA((4,)),
        ],
        compiler_params=pltpu.CompilerParams(vmem_limit_bytes=58 * 1024 * 1024),
    )(scan_offsets.T, grads)


def solution(mesh):
    return jax.shard_map(
        functools.partial(body, count=mesh.shape["depth"]),
        mesh=mesh,
        in_specs=(
            P(("groups", "depth"), None, None, None),
            P("groups", None, None, None),
            P("groups", None, None),
            P("groups", None),
            P("groups"),
        ),
        out_specs=P(("groups", "depth"), None, None, None),
        check_vma=False,
    )
```

```python
import functools
import math

import jax
import jax.numpy as jnp
import ml_dtypes
import numpy as np
from jax import lax
from jax.experimental import pallas as pl
from jax.experimental.pallas import tpu as pltpu
from jax.sharding import PartitionSpec as P

MESH = pl.DeviceIdType.MESH


def split_table(table):
    high = table.astype(ml_dtypes.bfloat16)
    low = (table - high.astype(np.float64)).astype(ml_dtypes.bfloat16)
    return np.stack([high, low])


def right_left(matrix):
    real, imag = matrix.real, matrix.imag
    right = np.block([[real, imag], [-imag, real]])
    left = np.block([[real, -imag], [imag, real]])
    return np.stack([split_table(right), split_table(left)])


def tables(length):
    ordinal = np.arange(length)
    dft = np.exp(-2j * math.pi * (np.outer(ordinal, ordinal) % length) / length) / math.sqrt(length)
    spatial = np.where(ordinal < length // 2, ordinal, ordinal - length)
    chirp = np.exp(-1j * math.pi * (spatial * spatial % (2 * length)) / length)
    prop = (dft.conj() * chirp[None, :]) @ dft
    return np.stack([right_left(prop), right_left(dft)])


def split(values):
    high = values.astype(jnp.bfloat16)
    low = (values - high.astype(jnp.float32)).astype(jnp.bfloat16)
    return high, low


def dot(left, right):
    return jnp.dot(left, right, preferred_element_type=jnp.float32)


def two_sided(real, imag, table_ref, which):
    length = real.shape[0]
    high, low = split(jnp.concatenate([real, imag], axis=1))
    both = dot(jnp.concatenate([high, low], axis=0), table_ref[which, 0, 0])
    mid = both[:length] + both[length:] + dot(high, table_ref[which, 0, 1])
    stacked = jnp.concatenate([mid[:, :length], mid[:, length:]], axis=0)
    high, low = split(stacked)
    both = dot(table_ref[which, 1, 0], jnp.concatenate([high, low], axis=1))
    out = both[:, :length] + both[:, length:] + dot(table_ref[which, 1, 1], high)
    return out[:length], out[length:]


def complex_mul(left_real, left_imag, right_real, right_imag):
    return (
        left_real * right_real - left_imag * right_imag,
        left_real * right_imag + left_imag * right_real,
    )


def one_hot(length, width, start, axis):
    shape = (length, width) if axis == 0 else (width, length)
    place = lax.broadcasted_iota(jnp.int32, shape, axis)
    wanted = lax.broadcasted_iota(jnp.int32, shape, 1 - axis) + start
    return jnp.where(place == wanted, 1.0, 0.0).astype(jnp.bfloat16)


def chain_kernel(
    count, shift, offsets, ids, obj_hbm, probes_hbm, measured_hbm, table_hbm,
    grads,
    table, obj, probes, measured, windows, win_in, waves, back_buf, grad_out, hop_out, hop_in,
    win_send, win_recv, grad_send, grad_recv, hop_send, hop_recv, load_sem,
):
    positions, window = measured_hbm.shape[0], measured_hbm.shape[-1]
    me = lax.axis_index("depth")
    mine = lax.rem(me, positions)
    segment = me // positions
    last = count // positions - 1

    loads = [
        pltpu.make_async_copy(source, target, load_sem.at[i])
        for i, (source, target) in enumerate((
            (obj_hbm.at[0], obj), (table_hbm, table), (probes_hbm, probes),
            (measured_hbm.at[mine], measured),
        ))
    ]
    for load in loads:
        load.start()

    def lead(place):
        return shift * (1 - 2 * lax.rem(place, 2))

    def begin(part, place):
        return jnp.where(part == 0, 0, part * positions - lead(place))

    def holder(place):
        return jnp.minimum(jnp.maximum(me + lead(place), 0) // positions, last)

    low = begin(segment, mine)
    slots = jnp.where(segment == last, count, begin(segment + 1, mine)) - low
    keeps = holder(mine) == segment
    early = (lax.rem(mine, 2) == 0) & (segment > 0)
    held_back = jnp.where(early, shift, 0)

    barrier = pltpu.get_barrier_semaphore()

    def greet(peer):
        pl.semaphore_signal(barrier, inc=1, device_id={"depth": peer}, device_id_type=MESH)

    def greet_owner(slot, carry):
        @pl.when(low + slot != me)
        def _():
            greet(low + slot)

        return carry

    lax.fori_loop(0, slots, greet_owner, 0)
    for step in range(1, positions):
        place = lax.rem(mine + step, positions)
        greet(holder(place) * positions + place)

    @pl.when(jnp.logical_not(keeps))
    def _():
        greet(holder(mine) * positions + mine)

    @pl.when(segment < last)
    def _():
        greet(me + positions)

    @pl.when(segment > 0)
    def _():
        greet(me - positions)

    greetings = (
        slots + positions - jnp.where(keeps, 2, 0)
        + jnp.where(segment < last, 1, 0) + jnp.where(segment > 0, 1, 0)
    )

    def win_copy(place):
        part = holder(place)
        slot = me - begin(part, place)
        return pltpu.make_async_remote_copy(
            src_ref=windows.at[place], dst_ref=win_in.at[slot],
            send_sem=win_send.at[place], recv_sem=win_recv.at[slot],
            device_id={"depth": part * positions + place}, device_id_type=MESH,
        )

    loads[0].wait()
    side = obj.shape[-1]
    field = obj[...].reshape(2 * side, side)
    half = positions // 2

    def order(turn):
        return 2 * lax.rem(mine // 2 + 1 + turn % half, half) + turn // half

    def ship(place):
        @pl.when(jnp.logical_not(keeps & (place == mine)))
        def _():
            win_copy(place).start()

        @pl.when(keeps & (place == mine))
        def _():
            win_in[me - low] = windows[place]

    def shipped(place):
        @pl.when(jnp.logical_not(keeps & (place == mine)))
        def _():
            win_copy(place).wait_send()

    for pair in range(0, positions, 2):
        places = [order(pair), order(pair + 1)]
        across = [one_hot(side, window, offsets[1, place], 0) for place in places]
        strips = dot(field, jnp.concatenate(across, axis=1)).astype(jnp.bfloat16)
        for i, place in enumerate(places):
            strip = strips[:, i * window : (i + 1) * window]
            strip = jnp.concatenate([strip[:side], strip[side:]], axis=1)
            tile = dot(one_hot(side, window, offsets[0, place], 1), strip)
            windows[place, 0] = tile[:, :window]
            windows[place, 1] = tile[:, window:]
        if pair == 0:
            pl.semaphore_wait(barrier, greetings)
        if pair < half:
            for place in places:
                ship(place)
    for turn in range(half):
        shipped(order(turn))
    for turn in range(half, positions):
        ship(order(turn))

    for load in loads[1:]:
        load.wait()

    def hop(which, peer):
        return pltpu.make_async_remote_copy(
            src_ref=hop_out.at[which], dst_ref=hop_in.at[which],
            send_sem=hop_send.at[which], recv_sem=hop_recv.at[which],
            device_id={"depth": peer}, device_id_type=MESH,
        )

    @pl.when(segment == 0)
    def _():
        chosen = ids[mine]
        wave = jnp.zeros(probes.shape[1:], jnp.float32)
        for which in range(probes.shape[0]):
            wave = jnp.where(chosen == which, probes[which], wave)
        waves[0] = wave

    @pl.when(segment > 0)
    def _():
        hop(0, me - positions).wait_recv()
        waves[0] = hop_in[0]

    def win_wait(slot):
        @pl.when(low + slot != me)
        def _():
            pltpu.make_async_remote_copy(
                src_ref=windows.at[0], dst_ref=win_in.at[slot],
                send_sem=win_send.at[0], recv_sem=win_recv.at[slot],
                device_id={"depth": low + slot}, device_id_type=MESH,
            ).wait_recv()

    def exit_wave(slot):
        return complex_mul(waves[slot, 0], waves[slot, 1], win_in[slot, 0], win_in[slot, 1])

    def advance(slot):
        real, imag = two_sided(*exit_wave(slot), table, 0)
        waves[slot + 1, 0] = real
        waves[slot + 1, 1] = imag

    def forward(pair, carry):
        win_wait(2 * pair + 1)
        win_wait(2 * pair + 2)
        advance(2 * pair + 1)
        advance(2 * pair + 2)
        return carry

    win_wait(0)
    advance(0)
    lax.fori_loop(0, slots // 2 - 1, forward, 0)
    win_wait(slots - 1)

    @pl.when(segment < last)
    def _():
        real, imag = two_sided(*exit_wave(slots - 1), table, 0)
        hop_out[0, 0] = real
        hop_out[0, 1] = imag
        hop(0, me + positions).start()
        hop(1, me + positions).wait_recv()
        back_buf[0] = hop_in[1, 0]
        back_buf[1] = hop_in[1, 1]

    @pl.when(segment == last)
    def _():
        far_real, far_imag = two_sided(*exit_wave(slots - 1), table, 1)
        excess = far_real * far_real + far_imag * far_imag - measured[...]
        real, imag = two_sided(excess * far_real, -(excess * far_imag), table, 1)
        back_buf[0] = real
        back_buf[1] = imag

    def grad_copy(slot):
        return pltpu.make_async_remote_copy(
            src_ref=grad_out.at[slot], dst_ref=grads.at[mine],
            send_sem=grad_send.at[slot], recv_sem=grad_recv.at[mine],
            device_id={"depth": low + slot}, device_id_type=MESH,
        )

    def keep_copy(slot):
        return pltpu.make_async_copy(grad_out.at[slot], grads.at[mine], load_sem.at[0])

    def keep_term(slot):
        real, imag = complex_mul(waves[slot, 0], waves[slot, 1], back_buf[0], back_buf[1])
        grad_out[slot, 0] = real
        grad_out[slot, 1] = -imag

    def give(slot):
        @pl.when(low + slot == me)
        def _():
            keep_copy(slot).start()

        @pl.when((low + slot != me) & (slot >= held_back))
        def _():
            grad_copy(slot).start()

    def send_back(slot):
        return two_sided(
            *complex_mul(win_in[slot, 0], win_in[slot, 1], back_buf[0], back_buf[1]), table, 0
        )

    def backward(step, carry):
        slot = slots - 1 - step
        keep_term(slot)
        real, imag = send_back(slot)
        back_buf[0] = real
        back_buf[1] = imag
        give(slot)
        return carry

    lax.fori_loop(0, slots - 1, backward, 0)
    keep_term(0)
    give(0)

    @pl.when(segment > 0)
    def _():
        real, imag = send_back(0)
        hop_out[1, 0] = real
        hop_out[1, 1] = imag
        hop(1, me - positions).start()
        hop(1, me - positions).wait_send()

    @pl.when(segment < last)
    def _():
        hop(0, me + positions).wait_send()

    @pl.when(early)
    def _():
        for slot in range(shift):
            grad_copy(slot).start()

    def sent(slot, carry):
        @pl.when(low + slot != me)
        def _():
            grad_copy(slot).wait_send()

        @pl.when(low + slot == me)
        def _():
            keep_copy(slot).wait()

        return carry

    lax.fori_loop(0, slots, sent, 0)

    for turn in range(half, positions):
        shipped(order(turn))

    def landed(place):
        pltpu.make_async_remote_copy(
            src_ref=grad_out.at[0], dst_ref=grads.at[place],
            send_sem=grad_send.at[0], recv_sem=grad_recv.at[place],
            device_id={"depth": holder(place) * positions + place}, device_id_type=MESH,
        ).wait_recv()

    for step in range(1, positions):
        landed(lax.rem(mine + step, positions))

    @pl.when(jnp.logical_not(keeps))
    def _():
        landed(mine)


def paint_kernel(offsets, grads_hbm, out_hbm, grads, out, total, load_sem, store_sem):
    positions, window = grads.shape[0], grads.shape[-1]
    side = out.shape[-1]
    loads = [
        pltpu.make_async_copy(grads_hbm.at[i], grads.at[i], load_sem.at[i]) for i in range(positions)
    ]
    for load in loads:
        load.start()
    total[...] = jnp.zeros_like(total)
    tall, wide = window + 8, 2 * window
    for position in range(positions):
        loads[position].wait()
        row, col = offsets[0, position], offsets[1, position]
        row_base = jnp.minimum((row >> 3) << 3, side - tall)
        col_base = jnp.minimum(col // window * window, side - wide)
        rows = pl.ds(pl.multiple_of(row_base, 8), tall)
        cols = pl.ds(pl.multiple_of(col_base, 128), wide)
        for part in range(2):
            tile = grads[position, part]
            tile = jnp.concatenate([tile, jnp.zeros((8, window), jnp.float32)], axis=0)
            tile = pltpu.roll(tile, row - row_base, 0)
            tile = jnp.concatenate([tile, jnp.zeros((tall, window), jnp.float32)], axis=1)
            tile = pltpu.roll(tile, col - col_base, 1)
            total[part, rows, cols] += tile
    pieces = store_sem.shape[0]
    tall = side // pieces
    stores = []
    for piece in range(pieces):
        rows = pl.ds(piece * tall, tall)
        out[:, rows] = total[:, rows].astype(out.dtype)
        stores.append(
            pltpu.make_async_copy(out.at[:, rows], out_hbm.at[0, :, rows], store_sem.at[piece])
        )
        stores[-1].start()
    for store in stores:
        store.wait()


def body(object_slices, probes, measured, scan_offsets, probe_ids, *, count):
    positions, window = measured.shape[0], measured.shape[-1]
    side = object_slices.shape[-1]
    assert count % positions == 0 and positions % 8 == 0
    table = jnp.asarray(tables(window))
    smem = pl.BlockSpec(memory_space=pltpu.SMEM)
    field = (2, window, window)
    shift = 0
    stack = pltpu.VMEM((positions,) + field, jnp.float32)
    chain = pltpu.VMEM((positions + shift,) + field, jnp.float32)
    sems = pltpu.SemaphoreType.DMA((positions,))
    chain_sems = pltpu.SemaphoreType.DMA((positions + shift,))
    hbm = pl.BlockSpec(memory_space=pltpu.HBM)
    grads = pl.pallas_call(
        functools.partial(chain_kernel, count, shift),
        out_shape=jax.ShapeDtypeStruct((positions,) + field, jnp.float32),
        in_specs=[smem, smem, hbm, hbm, hbm, hbm],
        out_specs=hbm,
        scratch_shapes=[
            pltpu.VMEM(table.shape, jnp.bfloat16),
            pltpu.VMEM(object_slices.shape[1:], jnp.bfloat16),
            pltpu.VMEM(probes.shape, jnp.float32),
            pltpu.VMEM((window, window), jnp.float32),
            stack, chain, chain,
            pltpu.VMEM(field, jnp.float32),
            chain,
            pltpu.VMEM((2,) + field, jnp.float32),
            pltpu.VMEM((2,) + field, jnp.float32),
            sems, chain_sems, chain_sems, sems,
            pltpu.SemaphoreType.DMA((2,)),
            pltpu.SemaphoreType.DMA((2,)),
            pltpu.SemaphoreType.DMA((4,)),
        ],
        compiler_params=pltpu.CompilerParams(
            collective_id=0, has_side_effects=True, vmem_limit_bytes=58 * 1024 * 1024
        ),
    )(scan_offsets.T, probe_ids, object_slices, probes, measured, table)
    return pl.pallas_call(
        paint_kernel,
        out_shape=jax.ShapeDtypeStruct(object_slices.shape, jnp.bfloat16),
        in_specs=[smem, hbm],
        out_specs=hbm,
        scratch_shapes=[
            stack,
            pltpu.VMEM((2, side, side), jnp.bfloat16),
            pltpu.VMEM((2, side, side), jnp.float32),
            sems,
            pltpu.SemaphoreType.DMA((4,)),
        ],
        compiler_params=pltpu.CompilerParams(vmem_limit_bytes=58 * 1024 * 1024),
    )(scan_offsets.T, grads)


def solution(mesh):
    return jax.shard_map(
        functools.partial(body, count=mesh.shape["depth"]),
        mesh=mesh,
        in_specs=(
            P(("groups", "depth"), None, None, None),
            P("groups", None, None, None),
            P("groups", None, None),
            P("groups", None),
            P("groups"),
        ),
        out_specs=P(("groups", "depth"), None, None, None),
        check_vma=False,
    )
```
